128 devices in a mesh: req: 64 (over x, z, y), head: 2 (over core).
Axes of the slice: x: 4, y: 4, z: 4, core: 2. Of those that a mesh axis runs over, the one named last changes fastest.
Arguments:
- layer_input: bfloat16 [8192, 4096], P('req'), may hold values from -6 to 6
- q_proj: bfloat16 [4096, 4096], P('req', 'head'), may hold values from -0.09375 to 0.09375
- key_proj: bfloat16 [4096, 256], P(None, 'head'), may hold values from -0.09375 to 0.09375
- value_proj: bfloat16 [4096, 256], P(None, 'head'), may hold values from -0.09375 to 0.09375
- query_gain: float32 [128], replicated, may hold values from 0.1 to 1.9
- key_gain: float32 [128], replicated, may hold values from 0.1 to 1.9
- attn_gain: float32 [4096], replicated, may hold values from 0.1 to 1.9
- moe_gain: float32 [4096], replicated, may hold values from 0.1 to 1.9
- router: bfloat16 [4096, 128], replicated, may hold values from -0.09375 to 0.09375
- expert_ids: int32 [8192, 8], P(('req', 'head')), may hold values from 0 to 127, all different within a row; in each aligned block of 64 rows (0 to 63, 64 to 127, ...) at most 5 rows name the same one
- req_lengths: int32 [64, 4], P('req'), may hold values from 1 to 64, 128 in all within a row
- w_gate: bfloat16 [128, 4096, 768], P(('req', 'head')), may hold values from -0.09375 to 0.09375
- w_up: bfloat16 [128, 4096, 768], P(('req', 'head')), may hold values from -0.09375 to 0.09375
- w_down: bfloat16 [128, 768, 4096], P(('req', 'head')), may hold values from -0.21875 to 0.21875
- cotangent: bfloat16 [8192, 4096], P(('req', 'head')), may hold values from -6 to 6
Outputs:
- mixed: bfloat16 [8192, 4096], P(('req', 'head'))
- attribution: float32 [8192, 4096], P('req', 'head')
- token_score: float32 [8192], P('req')
The draws below stay inside these ranges and needn't reach their ends.
Inputs may be any that keep to these rules, and one draw needn't show every extreme that they name: `expert_ids`: each row names 8 different experts; in each aligned block of 64 rows no expert is named more than 5 times, a bound that some block reaches. `req_lengths`: each row sums to 128, and its largest entry is exactly 64.
All inputs are finite; a program needn't handle non-finite values.
Results may differ from the reference program's by a relative error of at most 0.008.
Values may be sent and summed in bfloat16 or wider, within the bound.
No kernel may reach another device: no remote copies, remote signals or barrier semaphores. Data moves between devices by JAX's collectives and lax.ppermute only.
A program may use at most 192 MiB of HBM per device.

```python
import math
import jax
import jax.numpy as jnp
import numpy as np
from jax import lax

D = 4096
HD = 128
QH = 32
KVH = 2
F = 768
TOP = 8
REQ_DEV = 4
TOK_REQ = 128
TOK_MOE = 64
E = 128
CAP = 5
TOKENS = 8192
N_REQ = 64
N_HEAD = 2


def block_scale(own_key, dims, split, smallest, largest):
    def one(axis_at, shards_of):
        steps = jax.random.uniform(jax.random.fold_in(jax.random.fold_in(own_key, 6), axis_at), (shards_of,), jnp.float32, smallest / len(split), largest / len(split))
        return jnp.repeat(jnp.exp(steps), dims[axis_at] // shards_of).reshape((-1,) + (1,) * (len(dims) - axis_at - 1))

    factor_of = one(*split[0])
    for cut in split[1:]:
        factor_of = factor_of * one(*cut)
    return factor_of


def profile(amount, total, limit, lean):
    portions = [(1 << 20) // math.isqrt(standing ** lean) + 1 for standing in range(2, amount + 1)]
    surplus, given = total - limit - (amount - 1), [1] * (amount - 1)
    while surplus > 0:
        candidates = [i for i in range(amount - 1) if given[i] < limit]
        mass, remaining = sum([portions[i] for i in candidates]), surplus
        for i in candidates:
            addition = min(limit - given[i], max(1, remaining * portions[i] // mass), surplus)
            given[i] = given[i] + addition
            surplus = surplus - addition
    return np.array([limit] + given)


def uneven(stream_key, count, total, reach, lean):
    if count == 2:
        one = jax.random.randint(stream_key, (), max(1, total - reach), min(reach, total - 1) + 1)
        return jnp.stack([one, total - one])
    sizes = jnp.asarray(profile(count, total, reach, lean), jnp.int32)
    pairs = (count - 1) // 2
    donor, taker = sizes[1:1 + 2 * pairs:2], sizes[2:2 + 2 * pairs:2]
    slack = jnp.minimum(donor - 1, reach - taker)
    moved = jax.random.randint(jax.random.fold_in(stream_key, 1), (pairs,), 0, 1 << 20) % (slack + 1)
    sizes = sizes.at[1:1 + 2 * pairs:2].set(donor - moved).at[2:2 + 2 * pairs:2].set(taker + moved)
    return sizes[jax.random.permutation(jax.random.fold_in(stream_key, 2), count)]


def shared_out(rng, own, number, rows, number_of, top, reach, slope):
    order = jax.random.permutation(rng, number_of)
    packed, ordinary = portions_of(number_of, rows * top, reach, slope, True), portions_of(number_of, rows * top, reach, slope, False)
    places = jnp.arange(number_of)

    def named(lengths, turn):
        used = int((lengths > 0).sum())
        fixed = max(1, used // 4)
        moved = fixed + (places - fixed + turn * (used - fixed)) % max(1, number_of - fixed)
        return jnp.zeros((number_of,), jnp.int32).at[order[jnp.where(places < fixed, places, moved)]].set(jnp.asarray(lengths, jnp.int32))

    lengths = jnp.where(number % 4 == 0, named(packed, number // 4), named(ordinary, number - number // 4 - 1))
    mixed = jax.random.permutation(jax.random.fold_in(own, 3), number_of)
    source_of, receiver = mixed[0:number_of // 2 * 2:2], mixed[1:number_of // 2 * 2:2]
    slack = jnp.minimum(lengths[source_of] - 1, reach - lengths[receiver]) // 2
    slack = jnp.where((source_of == order[0]) | (receiver == order[0]) | (lengths[receiver] == 0), 0, jnp.maximum(slack, 0))
    moved = jax.random.randint(jax.random.fold_in(own, 4), (number_of // 2,), 0, 1 << 20) % (slack + 1)
    lengths = lengths.at[source_of].add(-moved).at[receiver].add(moved)
    items = jnp.searchsorted(jnp.cumsum(lengths), jnp.arange(rows * top), side="right").astype(jnp.int32)
    grid = items.reshape(top, rows).T
    grid = grid[jax.random.permutation(jax.random.fold_in(own, 1), rows)]
    turn = jax.random.randint(jax.random.fold_in(own, 2), (rows, 1), 0, top)
    return jnp.take_along_axis(grid, (jnp.arange(top)[None, :] + turn) % top, axis=1)


def portions_of(number_of, total, most, slope, full):
    loads = [(1 << 20) // math.isqrt(rank ** slope) + 1 for rank in range(1, number_of + 1)]
    largest = most if full else min(most, max(-(-total // number_of), total * loads[0] // sum(loads)))
    least = 1 if total - largest >= number_of - 1 else 0
    holding, surplus = [largest] + [least] * (number_of - 1), total - largest - least * (number_of - 1)
    while surplus > 0:
        free = [i for i in range(1, number_of) if holding[i] < largest] or [i for i in range(1, number_of) if holding[i] < most]
        mass, left = sum([loads[i] for i in free]), surplus
        for i in free:
            addition = min(most - holding[i], max(1, left * loads[i] // mass), surplus)
            holding[i] = holding[i] + addition
            surplus = surplus - addition
    return np.array(holding)


def bell_draw(rng, shape, width, limit, cuts=(), held_as=jnp.bfloat16):
    drawn = jax.random.normal(rng, shape, jnp.float32) * width
    if len(cuts) > 0:
        drawn = block_scale(rng, shape, cuts, -0.22, 0.18) * drawn
    return jnp.clip(drawn, min=-limit, max=limit).astype(held_as)


def setup_inputs(seed: int = 0) -> dict:
    arg_keys = jax.random.split(jax.random.key(seed), 16)
    layer_input = bell_draw(arg_keys[0], (TOKENS, D), 1.0, 6.0, ((0, 64),))
    q_proj = bell_draw(arg_keys[1], (D, QH * HD), D ** -0.5, 0.09375, ((0, 64), (1, 2)))
    key_proj = bell_draw(arg_keys[2], (D, KVH * HD), D ** -0.5, 0.09375, ((1, 2),))
    value_proj = bell_draw(arg_keys[3], (D, KVH * HD), D ** -0.5, 0.09375, ((1, 2),))
    query_gain = jnp.clip(1.0 + 0.18 * jax.random.normal(arg_keys[4], (HD,), jnp.float32), 0.1, 1.9)
    key_gain = jnp.clip(1.0 + 0.18 * jax.random.normal(arg_keys[5], (HD,), jnp.float32), 0.1, 1.9)
    attn_gain = jnp.clip(1.0 + 0.18 * jax.random.normal(arg_keys[6], (D,), jnp.float32), 0.1, 1.9)
    moe_gain = jnp.clip(1.0 + 0.18 * jax.random.normal(arg_keys[7], (D,), jnp.float32), 0.1, 1.9)
    router = bell_draw(arg_keys[8], (D, E), D ** -0.5, 0.09375)
    expert_ids_keys = jax.random.split(jax.random.fold_in(arg_keys[9], 1), TOKENS // TOK_MOE)
    expert_ids_turns = jax.random.permutation(jax.random.fold_in(arg_keys[9], 3), TOKENS // TOK_MOE)
    expert_ids = jax.vmap(lambda own, number: shared_out(jax.random.fold_in(arg_keys[9], 2), own, number, TOK_MOE, E, TOP, CAP, 2))(expert_ids_keys, expert_ids_turns).reshape((TOKENS, TOP))
    req_lengths = jax.vmap(lambda own: uneven(own, REQ_DEV, TOK_REQ, TOK_REQ // 2, 2))(jax.random.split(arg_keys[10], N_REQ)).reshape((N_REQ, REQ_DEV)).astype(jnp.int32)
    w_gate = bell_draw(arg_keys[11], (E, D, F), D ** -0.5, 0.09375, ((0, 128),))
    w_up = bell_draw(arg_keys[12], (E, D, F), D ** -0.5, 0.09375, ((0, 128),))
    w_down = bell_draw(arg_keys[13], (E, F, D), F ** -0.5, 0.21875, ((0, 128),))
    cotangent = bell_draw(arg_keys[14], (TOKENS, D), 1.0, 6.0, ((0, 128),))
    return {"layer_input": layer_input, "q_proj": q_proj, "key_proj": key_proj, "value_proj": value_proj, "query_gain": query_gain, "key_gain": key_gain, "attn_gain": attn_gain, "moe_gain": moe_gain, "router": router, "expert_ids": expert_ids, "req_lengths": req_lengths, "w_gate": w_gate, "w_up": w_up, "w_down": w_down, "cotangent": cotangent}


EPS = 1e-06
THETA = 1000000.0
NEG = -1e+30

def segments_of(lengths_row, token_count):
    lengths_row = lengths_row.astype(jnp.int32)
    ends = jnp.cumsum(lengths_row).astype(jnp.int32)
    starts = (ends - lengths_row).astype(jnp.int32)
    places = jnp.arange(token_count, dtype=jnp.int32)
    segment = lax.optimization_barrier(jnp.sum((places[:, None] >= ends[None, :]).astype(jnp.int32), axis=1)).astype(jnp.int32)
    picked = (segment[:, None] == jnp.arange(lengths_row.shape[0], dtype=jnp.int32)[None, :]).astype(jnp.int32)
    start_of = lax.optimization_barrier(jnp.sum(picked * starts[None, :], axis=1)).astype(jnp.int32)
    return (segment, places - start_of)

def rope_tables(offsets, half_dim):
    freq = THETA ** (-jnp.arange(half_dim, dtype=jnp.float32) / half_dim)
    angle = offsets.astype(jnp.float32)[:, None] * freq[None, :]
    return (jnp.cos(angle), jnp.sin(angle))

def rotate(rows, cosine_table, sine_table):
    half_dim = rows.shape[-1] // 2
    first = rows[..., :half_dim]
    second = rows[..., half_dim:]
    return jnp.concatenate([first * cosine_table - second * sine_table, second * cosine_table + first * sine_table], axis=-1)

def unrotate(rows, cosine_table, sine_table):
    half_dim = rows.shape[-1] // 2
    first = rows[..., :half_dim]
    second = rows[..., half_dim:]
    return jnp.concatenate([first * cosine_table + second * sine_table, second * cosine_table - first * sine_table], axis=-1)

def rms_scale(values):
    return lax.rsqrt(lax.optimization_barrier(jnp.mean(values * values, axis=-1, keepdims=True)) + EPS)

def norm_backward(values, scale, gain, grad_out):
    weighted = grad_out * gain
    inner = lax.optimization_barrier(jnp.mean(weighted * values, axis=-1, keepdims=True))
    return scale * weighted - values * scale ** 3 * inner

def attend_forward(normed, query_w, key_w, value_w, query_gain, key_gain, segment, offsets):
    head_dim = key_w.shape[1]
    token_count = normed.shape[0]
    groups = query_w.shape[1] // head_dim
    cosine_table, sine_table = rope_tables(offsets, head_dim // 2)
    query_raw = jnp.dot(normed, query_w, preferred_element_type=jnp.float32).reshape(token_count, groups, head_dim)
    query_scale = rms_scale(query_raw)
    query_normed = query_raw * query_scale * query_gain.astype(jnp.float32)
    queries3 = rotate(query_normed, cosine_table[:, None, :], sine_table[:, None, :]).astype(jnp.bfloat16)
    key_raw = jnp.dot(normed, key_w, preferred_element_type=jnp.float32)
    key_scale = rms_scale(key_raw)
    key_normed = key_raw * key_scale * key_gain.astype(jnp.float32)
    key_rows = rotate(key_normed, cosine_table, sine_table).astype(jnp.bfloat16)
    value_rows = jnp.dot(normed, value_w, preferred_element_type=jnp.float32).astype(jnp.bfloat16)
    factor = 1.0 / math.sqrt(head_dim)
    scores = jnp.einsum('qgd,kd->gqk', queries3.astype(jnp.float32), key_rows.astype(jnp.float32)) * factor
    places = jnp.arange(token_count, dtype=jnp.int32)
    allowed = (segment[:, None] == segment[None, :]) & (places[None, :] <= places[:, None])
    scores = jnp.where(allowed[None, :, :], scores, NEG)
    exponent_terms = jnp.exp(scores)
    attn_weights = exponent_terms / lax.optimization_barrier(jnp.sum(exponent_terms, axis=2, keepdims=True))
    attn_rounded = attn_weights.astype(jnp.bfloat16)
    context = jnp.einsum('gqk,kd->qgd', attn_rounded.astype(jnp.float32), value_rows.astype(jnp.float32))
    context = context.astype(jnp.bfloat16).reshape(token_count, groups * head_dim)
    saved = (query_raw, query_scale, key_raw, key_scale, key_rows, cosine_table, sine_table, value_rows, queries3, attn_weights, attn_rounded)
    return (context, saved)

def attend_backward(grad_context, saved, query_w, key_w, value_w, query_gain, key_gain):
    query_raw, query_scale, key_raw, key_scale, key_rows, cosine_table, sine_table, value_rows, queries3, attn_weights, attn_rounded = saved
    token_count, groups, head_dim = queries3.shape
    factor = 1.0 / math.sqrt(head_dim)
    grad_rounded = grad_context.astype(jnp.bfloat16).reshape(token_count, groups, head_dim).astype(jnp.float32)
    grad_weights = jnp.einsum('qgd,kd->gqk', grad_rounded, value_rows.astype(jnp.float32))
    grad_values = jnp.einsum('gqk,qgd->kd', attn_rounded.astype(jnp.float32), grad_rounded)
    centered = grad_weights - lax.optimization_barrier(jnp.sum(grad_weights * attn_weights, axis=2, keepdims=True))
    grad_scores = (attn_weights * centered * factor).astype(jnp.bfloat16)
    grad_keys = jnp.einsum('gqk,qgd->kd', grad_scores.astype(jnp.float32), queries3.astype(jnp.float32))
    grad_key_normed = unrotate(grad_keys, cosine_table, sine_table)
    grad_raw = norm_backward(key_raw, key_scale, key_gain.astype(jnp.float32), grad_key_normed)
    grad_queries = jnp.einsum('gqk,kd->qgd', grad_scores.astype(jnp.float32), key_rows.astype(jnp.float32))
    grad_query_normed = unrotate(grad_queries, cosine_table[:, None, :], sine_table[:, None, :])
    grad_query_raw = norm_backward(query_raw, query_scale, query_gain.astype(jnp.float32), grad_query_normed)
    grad_query_raw = grad_query_raw.reshape(token_count, groups * head_dim).astype(jnp.bfloat16)
    return jnp.dot(grad_query_raw, query_w.T, preferred_element_type=jnp.float32) + jnp.dot(grad_raw.astype(jnp.bfloat16), key_w.T, preferred_element_type=jnp.float32) + jnp.dot(grad_values.astype(jnp.bfloat16), value_w.T, preferred_element_type=jnp.float32)

def expert_backward(grad_out, pre_gate, pre_up, gate_w, up_w, down_w):
    grad_hidden = jnp.dot(grad_out, down_w.T, preferred_element_type=jnp.float32)
    sigmoid_gate = jax.nn.sigmoid(pre_gate)
    grad_up = (grad_hidden * pre_gate * sigmoid_gate).astype(jnp.bfloat16)
    grad_gate = (grad_hidden * pre_up * sigmoid_gate * (1.0 + pre_gate * (1.0 - sigmoid_gate))).astype(jnp.bfloat16)
    total = jnp.dot(grad_gate, gate_w.T, preferred_element_type=jnp.float32) + jnp.dot(grad_up, up_w.T, preferred_element_type=jnp.float32)
    return total.astype(jnp.bfloat16)

def reference(layer_input, q_proj, key_proj, value_proj, query_gain, key_gain, attn_gain, moe_gain, router, expert_ids, req_lengths, w_gate, w_up, w_down, cotangent):
    group_width = QH // KVH * HD
    attn_gain32 = attn_gain.astype(jnp.float32)
    blocks = layer_input.reshape(N_REQ, TOK_REQ, D)

    def attention_norm(block):
        block32 = block.astype(jnp.float32)
        scale = rms_scale(block32)
        return (block32, scale, (block32 * scale * attn_gain32[None, :]).astype(jnp.bfloat16))

    def forward_block(operands):
        block, lengths_row = operands
        segment, offsets = segments_of(lengths_row, TOK_REQ)
        block32, scale, normed = attention_norm(block)
        pieces = []
        for group_index in range(KVH):
            key_cols = key_proj[:, group_index * HD:(group_index + 1) * HD]
            value_cols = value_proj[:, group_index * HD:(group_index + 1) * HD]
            query_cols = q_proj[:, group_index * group_width:(group_index + 1) * group_width]
            context, saved = attend_forward(normed, query_cols, key_cols, value_cols, query_gain, key_gain, segment, offsets)
            pieces.append(context)
        return jnp.concatenate(pieces, axis=1)
    context = lax.map(forward_block, (blocks, req_lengths)).reshape(TOKENS, D)
    residual = layer_input.astype(jnp.float32) + context.astype(jnp.float32)
    moe_scale = rms_scale(residual)
    moe_gain32 = moe_gain.astype(jnp.float32)
    moe_in = (residual * moe_scale * moe_gain32[None, :]).astype(jnp.bfloat16)
    logits = jnp.dot(moe_in, router, preferred_element_type=jnp.float32)
    chosen = jnp.take_along_axis(logits, expert_ids, axis=1)
    gates = jax.nn.softmax(chosen, axis=1)
    cot32 = cotangent.astype(jnp.float32)
    flat_ids = expert_ids.reshape(-1)
    flat_gates = gates.reshape(-1)
    rows_most = N_REQ * N_HEAD * CAP

    def per_expert(carry, operands):
        moe_sum, grad_in, gate_grad = carry
        expert, gate_w, up_w, down_w = operands
        hits = flat_ids == expert
        picked = jnp.nonzero(hits, size=rows_most, fill_value=0)[0].astype(jnp.int32)
        live = jnp.arange(rows_most, dtype=jnp.int32) < jnp.sum(hits.astype(jnp.int32))
        owner = picked // TOP
        rows_in = moe_in[owner]
        pre_gate = jnp.dot(rows_in, gate_w, preferred_element_type=jnp.float32)
        pre_up = jnp.dot(rows_in, up_w, preferred_element_type=jnp.float32)
        hidden = (jax.nn.silu(pre_gate) * pre_up).astype(jnp.bfloat16)
        outputs = jnp.dot(hidden, down_w, preferred_element_type=jnp.float32).astype(jnp.bfloat16)
        slot_gate = flat_gates[picked]
        cot_rows = cot32[owner]
        grad_out = (slot_gate[:, None] * cot_rows).astype(jnp.bfloat16)
        grad_rows = expert_backward(grad_out, pre_gate, pre_up, gate_w, up_w, down_w)
        out32 = outputs.astype(jnp.float32)
        keep = live[:, None]
        moe_sum = moe_sum.at[owner].add(jnp.where(keep, slot_gate[:, None] * out32, 0.0))
        grad_in = grad_in.at[owner].add(jnp.where(keep, grad_rows.astype(jnp.float32), 0.0))
        gate_grad = gate_grad.at[picked].add(jnp.where(live, lax.optimization_barrier(jnp.sum(cot_rows * out32, axis=1)), 0.0))
        return ((moe_sum, grad_in, gate_grad), None)
    start = (jnp.zeros((TOKENS, D), jnp.float32), jnp.zeros((TOKENS, D), jnp.float32), jnp.zeros((TOKENS * TOP,), jnp.float32))
    experts_range = jnp.arange(E, dtype=jnp.int32)
    (moe_sum, grad_in, gate_grad), _ = lax.scan(per_expert, start, (experts_range, w_gate, w_up, w_down))
    mixed = (residual + moe_sum).astype(jnp.bfloat16)
    gate_grad = gate_grad.reshape(TOKENS, TOP)
    total_gate = lax.optimization_barrier(jnp.sum(gates * gate_grad, axis=1, keepdims=True))
    grad_logit = gates * (gate_grad - total_gate)
    dense = lax.optimization_barrier(jnp.sum(jnp.where(expert_ids[:, :, None] == experts_range[None, None, :], grad_logit[:, :, None], 0.0), axis=1))
    grad_in = grad_in + jnp.dot(dense, router.astype(jnp.float32).T, precision=lax.Precision.HIGHEST)
    grad_resid = cot32 + norm_backward(residual, moe_scale, moe_gain32, grad_in)
    grad_blocks = grad_resid.reshape(N_REQ, TOK_REQ, D)

    def backward_block(operands):
        block, lengths_row, grad_block = operands
        segment, offsets = segments_of(lengths_row, TOK_REQ)
        block32, scale, normed = attention_norm(block)
        grad_normed = jnp.zeros((TOK_REQ, D), jnp.float32)
        for group_index in range(KVH):
            key_cols = key_proj[:, group_index * HD:(group_index + 1) * HD]
            value_cols = value_proj[:, group_index * HD:(group_index + 1) * HD]
            query_cols = q_proj[:, group_index * group_width:(group_index + 1) * group_width]
            context, saved = attend_forward(normed, query_cols, key_cols, value_cols, query_gain, key_gain, segment, offsets)
            grad_cols = grad_block[:, group_index * group_width:(group_index + 1) * group_width]
            grad_normed = grad_normed + attend_backward(grad_cols, saved, query_cols, key_cols, value_cols, query_gain, key_gain)
        grad_input = grad_block + norm_backward(block32, scale, attn_gain32, grad_normed)
        attribution = grad_input * block32
        return (attribution, lax.optimization_barrier(jnp.sum(attribution, axis=1)))
    attribution, token_score = lax.map(backward_block, (blocks, req_lengths, grad_blocks))
    return (mixed, attribution.reshape(TOKENS, D), token_score.reshape(TOKENS))
```

```python
import math

import jax
import jax.numpy as jnp
from jax import lax
from jax.experimental import pallas as pl
from jax.experimental.pallas import tpu as pltpu
from jax.sharding import PartitionSpec as P


EPS = 1e-06
THETA = 1000000.0
NEG = -1e30


def segments_of(lengths_row, token_count):
    ends = jnp.cumsum(lengths_row)
    starts = ends - lengths_row
    places = jnp.arange(token_count, dtype=jnp.int32)
    segment = jnp.sum((places[:, None] >= ends[None, :]).astype(jnp.int32), axis=1)
    picked = (
        segment[:, None] == jnp.arange(lengths_row.shape[0], dtype=jnp.int32)[None, :]
    ).astype(jnp.int32)
    start_of = jnp.sum(picked * starts[None, :], axis=1)
    return (segment, places - start_of)


def rope_tables(offsets, half_dim):
    freq = THETA ** (-jnp.arange(half_dim, dtype=jnp.float32) / half_dim)
    angle = offsets.astype(jnp.float32)[:, None] * freq[None, :]
    return (jnp.cos(angle), jnp.sin(angle))


def rotate(rows, cosine_table, sine_table):
    half_dim = rows.shape[-1] // 2
    first = rows[..., :half_dim]
    second = rows[..., half_dim:]
    return jnp.concatenate(
        [first * cosine_table - second * sine_table, second * cosine_table + first * sine_table],
        axis=-1,
    )


def unrotate(rows, cosine_table, sine_table):
    half_dim = rows.shape[-1] // 2
    first = rows[..., :half_dim]
    second = rows[..., half_dim:]
    return jnp.concatenate(
        [first * cosine_table + second * sine_table, second * cosine_table - first * sine_table],
        axis=-1,
    )


def rms_scale(values):
    return lax.rsqrt(jnp.mean(values * values, axis=-1, keepdims=True) + EPS)


def norm_backward(values, scale, gain, grad_out):
    weighted = grad_out * gain
    inner = jnp.mean(weighted * values, axis=-1, keepdims=True)
    return scale * weighted - values * scale**3 * inner


def attend_forward(normed, query_w, key_w, value_w, query_gain, key_gain, segment, offsets):
    head_dim = key_w.shape[1]
    token_count = normed.shape[0]
    groups = query_w.shape[1] // head_dim
    cosine_table, sine_table = rope_tables(offsets, head_dim // 2)
    query_raw = jnp.dot(normed, query_w, preferred_element_type=jnp.float32).reshape(
        token_count, groups, head_dim
    )
    query_scale = rms_scale(query_raw)
    query_normed = query_raw * query_scale * query_gain
    queries3 = rotate(query_normed, cosine_table[:, None, :], sine_table[:, None, :]).astype(
        jnp.bfloat16
    )
    key_raw = jnp.dot(normed, key_w, preferred_element_type=jnp.float32)
    key_scale = rms_scale(key_raw)
    key_normed = key_raw * key_scale * key_gain
    key_rows = rotate(key_normed, cosine_table, sine_table).astype(jnp.bfloat16)
    value_rows = jnp.dot(normed, value_w, preferred_element_type=jnp.float32).astype(jnp.bfloat16)
    factor = 1.0 / math.sqrt(head_dim)
    scores = (
        jnp.einsum("qgd,kd->gqk", queries3, key_rows, preferred_element_type=jnp.float32) * factor
    )
    places = jnp.arange(token_count, dtype=jnp.int32)
    allowed = (segment[:, None] == segment[None, :]) & (places[None, :] <= places[:, None])
    scores = jnp.where(allowed[None, :, :], scores, NEG)
    exponent_terms = jnp.exp(scores)
    attn_weights = exponent_terms / jnp.sum(exponent_terms, axis=2, keepdims=True)
    attn_rounded = attn_weights.astype(jnp.bfloat16)
    context = jnp.einsum(
        "gqk,kd->qgd", attn_rounded, value_rows, preferred_element_type=jnp.float32
    )
    context = context.astype(jnp.bfloat16).reshape(token_count, groups * head_dim)
    saved = (
        query_raw,
        query_scale,
        key_raw,
        key_scale,
        key_rows,
        cosine_table,
        sine_table,
        value_rows,
        queries3,
        attn_weights,
        attn_rounded,
    )
    return (context, saved)


def attend_backward(grad_context, saved, query_w, key_w, value_w, query_gain, key_gain):
    (
        query_raw,
        query_scale,
        key_raw,
        key_scale,
        key_rows,
        cosine_table,
        sine_table,
        value_rows,
        queries3,
        attn_weights,
        attn_rounded,
    ) = saved
    token_count, groups, head_dim = queries3.shape
    factor = 1.0 / math.sqrt(head_dim)
    grad_rounded = grad_context.astype(jnp.bfloat16).reshape(token_count, groups, head_dim)
    grad_weights = jnp.einsum(
        "qgd,kd->gqk", grad_rounded, value_rows, preferred_element_type=jnp.float32
    )
    grad_values = jnp.einsum(
        "gqk,qgd->kd", attn_rounded, grad_rounded, preferred_element_type=jnp.float32
    )
    centered = grad_weights - jnp.sum(grad_weights * attn_weights, axis=2, keepdims=True)
    grad_scores = (attn_weights * centered * factor).astype(jnp.bfloat16)
    grad_keys = jnp.einsum("gqk,qgd->kd", grad_scores, queries3, preferred_element_type=jnp.float32)
    grad_key_normed = unrotate(grad_keys, cosine_table, sine_table)
    grad_raw = norm_backward(key_raw, key_scale, key_gain, grad_key_normed)
    grad_queries = jnp.einsum(
        "gqk,kd->qgd", grad_scores, key_rows, preferred_element_type=jnp.float32
    )
    grad_query_normed = unrotate(grad_queries, cosine_table[:, None, :], sine_table[:, None, :])
    grad_query_raw = norm_backward(query_raw, query_scale, query_gain, grad_query_normed)
    grad_query_raw = grad_query_raw.reshape(token_count, groups * head_dim).astype(jnp.bfloat16)
    return (
        jnp.dot(grad_query_raw, query_w.T, preferred_element_type=jnp.float32)
        + jnp.dot(grad_raw.astype(jnp.bfloat16), key_w.T, preferred_element_type=jnp.float32)
        + jnp.dot(grad_values.astype(jnp.bfloat16), value_w.T, preferred_element_type=jnp.float32)
    )


SUB = 32


def pick_kernel(index_ref, rows_ref, out_ref):
    step_rows = out_ref.shape[0]
    base = pl.program_id(0) * step_rows

    def one(i, carry):
        out_ref[i] = rows_ref[index_ref[base + i]]
        return carry

    lax.fori_loop(0, step_rows, one, 0, unroll=8)


def pick_rows(rows3, index, step_rows=80):
    count = index.shape[0]
    _, sub, lanes = rows3.shape
    return pl.pallas_call(
        pick_kernel,
        out_shape=jax.ShapeDtypeStruct((count, sub, lanes), rows3.dtype),
        grid_spec=pltpu.PrefetchScalarGridSpec(
            num_scalar_prefetch=1,
            grid=(count // step_rows,),
            in_specs=[pl.BlockSpec(rows3.shape, lambda i, ids: (0, 0, 0))],
            out_specs=pl.BlockSpec((step_rows, sub, lanes), lambda i, ids: (i, 0, 0)),
        ),
        cost_estimate=pl.CostEstimate(
            flops=0, transcendentals=0, bytes_accessed=count * sub * lanes * 2
        ),
        name="pick_rows",
    )(index, rows3)


def mix_kernel(index_ref, gate_ref, rows_ref, after_ref, out_ref):
    del after_ref
    step_tokens = out_ref.shape[0]
    top = index_ref.shape[0] // (step_tokens * pl.num_programs(0))
    base = pl.program_id(0) * step_tokens

    def one(i, carry):
        at = (base + i) * top
        total = gate_ref[at] * rows_ref[index_ref[at]].astype(jnp.float32)
        for k in range(1, top):
            total = total + gate_ref[at + k] * rows_ref[index_ref[at + k]].astype(jnp.float32)
        out_ref[i] = total
        return carry

    lax.fori_loop(0, step_tokens, one, 0, unroll=2)


def mix_rows(rows3, index, gates, tokens, after, step_tokens=16):
    _, sub, lanes = rows3.shape
    return pl.pallas_call(
        mix_kernel,
        out_shape=jax.ShapeDtypeStruct((tokens, sub, lanes), jnp.float32),
        grid_spec=pltpu.PrefetchScalarGridSpec(
            num_scalar_prefetch=2,
            grid=(tokens // step_tokens,),
            in_specs=[
                pl.BlockSpec(rows3.shape, lambda i, ids, g: (0, 0, 0)),
                pl.BlockSpec(after.shape, lambda i, ids, g: (0, 0)),
            ],
            out_specs=pl.BlockSpec((step_tokens, sub, lanes), lambda i, ids, g: (i, 0, 0)),
        ),
        cost_estimate=pl.CostEstimate(
            flops=index.shape[0] * sub * lanes * 2,
            transcendentals=0,
            bytes_accessed=rows3.shape[0] * sub * lanes * 2,
        ),
        name="mix_rows",
    )(index, gates, rows3, after)


def spread_kernel(rows_ref, out_ref, wide):
    count, sub, lanes = rows_ref.shape
    wide[...] = rows_ref[...].astype(jnp.float32).reshape(count * sub, lanes)
    for c in range(sub):
        out_ref[:, c * lanes : (c + 1) * lanes] = wide[pl.ds(c, count, stride=sub), :].astype(
            out_ref.dtype
        )


def spread_rows(rows3, step_rows=64):
    count, sub, lanes = rows3.shape
    return pl.pallas_call(
        spread_kernel,
        out_shape=jax.ShapeDtypeStruct((count, sub * lanes), rows3.dtype),
        grid=(count // step_rows,),
        in_specs=[pl.BlockSpec((step_rows, sub, lanes), lambda i: (i, 0, 0))],
        out_specs=pl.BlockSpec((step_rows, sub * lanes), lambda i: (i, 0)),
        scratch_shapes=[pltpu.VMEM((step_rows * sub, lanes), jnp.float32)],
        cost_estimate=pl.CostEstimate(
            flops=0, transcendentals=0, bytes_accessed=4 * count * sub * lanes
        ),
        name="spread_rows",
    )(rows3)


def fold_kernel(rows_ref, out_ref, wide):
    count, sub, lanes = out_ref.shape
    for c in range(sub):
        wide[pl.ds(c, count, stride=sub), :] = rows_ref[:, c * lanes : (c + 1) * lanes].astype(
            jnp.float32
        )
    out_ref[...] = wide[...].reshape(count, sub, lanes).astype(out_ref.dtype)


def fold_rows(rows, step_rows=64):
    count, width = rows.shape
    lanes = width // SUB
    return pl.pallas_call(
        fold_kernel,
        out_shape=jax.ShapeDtypeStruct((count, SUB, lanes), jnp.bfloat16),
        grid=(count // step_rows,),
        in_specs=[pl.BlockSpec((step_rows, width), lambda i: (i, 0))],
        out_specs=pl.BlockSpec((step_rows, SUB, lanes), lambda i: (i, 0, 0)),
        scratch_shapes=[pltpu.VMEM((step_rows * SUB, lanes), jnp.float32)],
        cost_estimate=pl.CostEstimate(
            flops=0, transcendentals=0, bytes_accessed=4 * count * width
        ),
        name="fold_rows",
    )(rows)


def swap_heads(values):
    return lax.ppermute(values, "head", [(0, 1), (1, 0)])


def exchange(rows3, device_count):
    count, sub, lanes = rows3.shape
    packed = rows3.reshape(device_count, (count // device_count) * sub, lanes)
    moved = lax.all_to_all(packed, ("req", "head"), split_axis=0, concat_axis=0, tiled=True)
    return moved.reshape(count, sub, lanes)


def device_step(
    layer_input,
    q_proj,
    key_proj,
    value_proj,
    query_gain,
    key_gain,
    attn_gain,
    moe_gain,
    router,
    expert_ids,
    req_lengths,
    w_gate,
    w_up,
    w_down,
    cotangent,
):
    head_count = lax.axis_size("head")
    head_index = lax.axis_index("head")
    device_count = lax.axis_size("req") * head_count
    token_count, width = layer_input.shape
    moe_tokens = token_count // head_count
    half_width = width // head_count
    capacity = 5
    first_core = head_index == 0

    query_w = lax.all_gather(q_proj, "req", axis=0, tiled=True)

    expert_range = jnp.arange(device_count, dtype=jnp.int32)
    chosen_mask = expert_ids[:, :, None] == expert_range[None, None, :]
    member = jnp.any(chosen_mask, axis=1)
    token_range = jnp.arange(moe_tokens, dtype=jnp.int32)
    before = (token_range[:, None] > token_range[None, :]).astype(jnp.bfloat16)
    rank = jnp.dot(before, member.astype(jnp.bfloat16), preferred_element_type=jnp.float32)
    rank = rank.astype(jnp.int32)
    slot_of = jnp.sum(jnp.where(chosen_mask, rank[:, None, :], 0), axis=2)
    target = (expert_ids * capacity + slot_of).reshape(-1)
    slot_range = jnp.arange(capacity, dtype=jnp.int32)
    hit = member[:, :, None] & (rank[:, :, None] == slot_range[None, None, :])
    source = jnp.sum(jnp.where(hit, token_range[:, None, None], 0), axis=0).reshape(-1)

    cot_send = pick_rows(fold_rows(cotangent), source)
    cot_send, query_w = lax.optimization_barrier((cot_send, query_w))
    cot_rows3 = exchange(cot_send, device_count)

    segment, offsets = segments_of(req_lengths[0], token_count)
    input32 = layer_input.astype(jnp.float32)
    input_scale = rms_scale(input32)
    normed = (input32 * input_scale * attn_gain[None, :]).astype(jnp.bfloat16)
    context, saved = attend_forward(
        normed, query_w, key_proj, value_proj, query_gain, key_gain, segment, offsets
    )
    other_rows = lax.dynamic_slice_in_dim(context, (1 - head_index) * moe_tokens, moe_tokens, 0)
    own_rows = lax.dynamic_slice_in_dim(context, head_index * moe_tokens, moe_tokens, 0)
    came = swap_heads(other_rows)
    context_tok = jnp.concatenate(
        [jnp.where(first_core, own_rows, came), jnp.where(first_core, came, own_rows)], axis=1
    )
    own_input = lax.dynamic_slice_in_dim(layer_input, head_index * moe_tokens, moe_tokens, 0)
    residual = own_input.astype(jnp.float32) + context_tok.astype(jnp.float32)
    moe_scale = rms_scale(residual)
    moe_in = (residual * moe_scale * moe_gain[None, :]).astype(jnp.bfloat16)
    moe_send = pick_rows(fold_rows(moe_in), source)
    rows3 = exchange(moe_send, device_count)

    logits = jnp.dot(moe_in, router, preferred_element_type=jnp.float32)
    chosen = jnp.sum(jnp.where(chosen_mask, logits[:, None, :], 0.0), axis=2)
    gates = jax.nn.softmax(chosen, axis=1)
    flat_gates = gates.reshape(-1)
    cot32 = cotangent.astype(jnp.float32)

    gate_w = w_gate[0]
    up_w = w_up[0]
    down_w = w_down[0]
    cot_rows = spread_rows(cot_rows3)
    cot_hidden = jnp.dot(cot_rows, down_w.T, preferred_element_type=jnp.float32)
    cot_hidden = lax.optimization_barrier(cot_hidden)
    rows = spread_rows(rows3)
    pre_gate = jnp.dot(rows, gate_w, preferred_element_type=jnp.float32)
    pre_up = jnp.dot(rows, up_w, preferred_element_type=jnp.float32)
    sigmoid_gate = jax.nn.sigmoid(pre_gate)
    silu_gate = pre_gate * sigmoid_gate
    hidden = (silu_gate * pre_up).astype(jnp.bfloat16)
    slot_grad = jnp.sum(hidden.astype(jnp.float32) * cot_hidden, axis=1)
    grad_up = (cot_hidden * silu_gate).astype(jnp.bfloat16)
    grad_gate = (
        cot_hidden * pre_up * sigmoid_gate * (1.0 + pre_gate * (1.0 - sigmoid_gate))
    ).astype(jnp.bfloat16)
    slot_grad = jnp.pad(slot_grad.reshape(device_count, capacity), ((0, 0), (0, 128 - capacity)))
    slot_back = lax.all_to_all(
        slot_grad.reshape(device_count, 1, 128),
        ("req", "head"),
        split_axis=0,
        concat_axis=0,
        tiled=True,
    )
    slot_back = slot_back.reshape(device_count, 128)[:, :capacity]
    grad_made = jnp.dot(grad_gate, gate_w.T, preferred_element_type=jnp.float32) + jnp.dot(
        grad_up, up_w.T, preferred_element_type=jnp.float32
    )
    grad_send = fold_rows(grad_made.astype(jnp.bfloat16))
    grad_back = exchange(grad_send, device_count)
    outputs = jnp.dot(hidden, down_w, preferred_element_type=jnp.float32).astype(jnp.bfloat16)
    out_send = fold_rows(outputs)
    out_back = exchange(out_send, device_count)

    hit_grad = jnp.sum(jnp.where(hit, slot_back[None, :, :], 0.0), axis=2)
    gate_grad = jnp.sum(jnp.where(chosen_mask, hit_grad[:, None, :], 0.0), axis=2)
    total_gate = jnp.sum(gates * gate_grad, axis=1, keepdims=True)
    grad_logit = gates * (gate_grad - total_gate)
    dense = jnp.sum(jnp.where(chosen_mask, grad_logit[:, :, None], 0.0), axis=1)
    router_part = jnp.dot(
        dense, router.astype(jnp.float32).T, precision=lax.Precision.HIGHEST
    )
    router_part = lax.optimization_barrier(router_part)
    grad_in = mix_rows(grad_back, target, flat_gates, moe_tokens, router_part[:8, :128])
    grad_in = grad_in.reshape(moe_tokens, width)
    grad_in = grad_in + router_part
    grad_resid = cot32 + norm_backward(residual, moe_scale, moe_gain, grad_in)
    left, right = grad_resid[:, :half_width], grad_resid[:, half_width:]
    came_grad = swap_heads(jnp.where(first_core, right, left))
    own_grad = jnp.where(first_core, left, right)
    grad_heads = jnp.concatenate(
        [jnp.where(first_core, own_grad, came_grad), jnp.where(first_core, came_grad, own_grad)],
        axis=0,
    )
    grad_normed = attend_backward(
        grad_heads, saved, query_w, key_proj, value_proj, query_gain, key_gain
    )
    input_half = lax.dynamic_slice_in_dim(layer_input, head_index * half_width, half_width, 1)
    input_half = input_half.astype(jnp.float32)
    gain_half = lax.dynamic_slice_in_dim(attn_gain, head_index * half_width, half_width, 0)
    normed_left, normed_right = grad_normed[:, :half_width], grad_normed[:, half_width:]
    came_half = swap_heads(jnp.where(first_core, normed_right, normed_left).astype(jnp.bfloat16))
    own_half = jnp.where(first_core, normed_left, normed_right)
    weighted = (own_half + came_half.astype(jnp.float32)) * gain_half[None, :]
    inner_part = jnp.sum(weighted * input_half, axis=1)
    direct_part = jnp.sum(grad_heads * input_half, axis=1)
    parts = jnp.stack([inner_part, direct_part], axis=0)
    inner_sum, direct_sum = parts + swap_heads(parts)
    inner = inner_sum[:, None] / width
    grad_attn = input_scale * weighted - input_half * input_scale**3 * inner
    attribution = (grad_heads + grad_attn) * input_half
    square_sum = jnp.sum(input32 * input32, axis=1)
    scale_row = input_scale[:, 0]
    token_score = direct_sum + (
        scale_row * inner_sum - scale_row**3 * (inner_sum / width) * square_sum
    )
    moe_sum = mix_rows(out_back, target, flat_gates, moe_tokens, own_half[:8, :128]).reshape(moe_tokens, width)
    mixed = (residual + moe_sum).astype(jnp.bfloat16)
    return (mixed, attribution, token_score)


def solution(mesh):
    return jax.shard_map(
        device_step,
        mesh=mesh,
        in_specs=(
            P("req", None),
            P("req", "head"),
            P(None, "head"),
            P(None, "head"),
            P(),
            P(),
            P(),
            P(),
            P(),
            P(("req", "head"), None),
            P("req", None),
            P(("req", "head"), None, None),
            P(("req", "head"), None, None),
            P(("req", "head"), None, None),
            P(("req", "head"), None),
        ),
        out_specs=(P(("req", "head"), None), P("req", "head"), P("req")),
        check_vma=False,
    )
```

```python
import functools
import math

import jax
import jax.numpy as jnp
from jax import lax
from jax.experimental import pallas as pl
from jax.experimental.pallas import tpu as pltpu
from jax.sharding import PartitionSpec as P


EPS = 1e-06
THETA = 1000000.0
NEG = -1e30


def segments_of(lengths_row, token_count):
    ends = jnp.cumsum(lengths_row)
    starts = ends - lengths_row
    places = jnp.arange(token_count, dtype=jnp.int32)
    segment = jnp.sum((places[:, None] >= ends[None, :]).astype(jnp.int32), axis=1)
    picked = (
        segment[:, None] == jnp.arange(lengths_row.shape[0], dtype=jnp.int32)[None, :]
    ).astype(jnp.int32)
    start_of = jnp.sum(picked * starts[None, :], axis=1)
    return (segment, places - start_of)


def rope_tables(offsets, half_dim):
    freq = THETA ** (-jnp.arange(half_dim, dtype=jnp.float32) / half_dim)
    angle = offsets.astype(jnp.float32)[:, None] * freq[None, :]
    return (jnp.cos(angle), jnp.sin(angle))


def rotate(rows, cosine_table, sine_table):
    half_dim = rows.shape[-1] // 2
    first = rows[..., :half_dim]
    second = rows[..., half_dim:]
    return jnp.concatenate(
        [first * cosine_table - second * sine_table, second * cosine_table + first * sine_table],
        axis=-1,
    )


def rms_scale(values):
    return lax.rsqrt(jnp.mean(values * values, axis=-1, keepdims=True) + EPS)


def norm_backward(values, scale, gain, grad_out):
    weighted = grad_out * gain
    inner = jnp.mean(weighted * values, axis=-1, keepdims=True)
    return scale * weighted - values * scale**3 * inner


SUB = 32
VMEM_LIMIT = 56 * 1024 * 1024


def pick_kernel(index_ref, rows_ref, out_ref, folded):
    step_rows = out_ref.shape[0]
    base = pl.program_id(0) * step_rows

    @pl.when(pl.program_id(0) == 0)
    def _():
        folded[...] = rows_ref[...].reshape(folded.shape)

    def one(i, carry):
        out_ref[i] = folded[index_ref[base + i]]
        return carry

    lax.fori_loop(0, step_rows, one, 0, unroll=8)


def pick_rows(rows, index, step_rows=80):
    count = index.shape[0]
    tokens, width = rows.shape
    lanes = width // SUB
    return pl.pallas_call(
        pick_kernel,
        out_shape=jax.ShapeDtypeStruct((count, SUB, lanes), rows.dtype),
        grid_spec=pltpu.PrefetchScalarGridSpec(
            num_scalar_prefetch=1,
            grid=(count // step_rows,),
            in_specs=[pl.BlockSpec(rows.shape, lambda i, ids: (0, 0))],
            out_specs=pl.BlockSpec((step_rows, SUB, lanes), lambda i, ids: (i, 0, 0)),
            scratch_shapes=[pltpu.VMEM((tokens, SUB, lanes), rows.dtype)],
        ),
        cost_estimate=pl.CostEstimate(
            flops=0, transcendentals=0, bytes_accessed=count * width * 2
        ),
        name="pick_rows",
    )(index, rows)


def mix_kernel(index_ref, gate_ref, rows_ref, after_ref, out_ref):
    del after_ref
    step_tokens = out_ref.shape[0]
    top = index_ref.shape[0] // (step_tokens * pl.num_programs(0))
    base = pl.program_id(0) * step_tokens

    def one(i, carry):
        at = (base + i) * top
        total = gate_ref[at] * rows_ref[index_ref[at]].astype(jnp.float32)
        for k in range(1, top):
            total = total + gate_ref[at + k] * rows_ref[index_ref[at + k]].astype(jnp.float32)
        out_ref[i] = total
        return carry

    lax.fori_loop(0, step_tokens, one, 0, unroll=2)


def mix_rows(rows3, index, gates, tokens, after, step_tokens=16):
    _, sub, lanes = rows3.shape
    return pl.pallas_call(
        mix_kernel,
        out_shape=jax.ShapeDtypeStruct((tokens, sub, lanes), jnp.float32),
        grid_spec=pltpu.PrefetchScalarGridSpec(
            num_scalar_prefetch=2,
            grid=(tokens // step_tokens,),
            in_specs=[
                pl.BlockSpec(rows3.shape, lambda i, ids, g: (0, 0, 0)),
                pl.BlockSpec(after.shape, lambda i, ids, g: (0, 0)),
            ],
            out_specs=pl.BlockSpec((step_tokens, sub, lanes), lambda i, ids, g: (i, 0, 0)),
        ),
        cost_estimate=pl.CostEstimate(
            flops=index.shape[0] * sub * lanes * 2,
            transcendentals=0,
            bytes_accessed=rows3.shape[0] * sub * lanes * 2,
        ),
        name="mix_rows",
    )(index, gates, rows3, after)


def spread_kernel(rows_ref, out_ref):
    out_ref[...] = rows_ref[...].reshape(out_ref.shape)


def spread_rows(rows3, step_rows=128):
    count, sub, lanes = rows3.shape
    return pl.pallas_call(
        spread_kernel,
        out_shape=jax.ShapeDtypeStruct((count, sub * lanes), rows3.dtype),
        grid=(count // step_rows,),
        in_specs=[pl.BlockSpec((step_rows, sub, lanes), lambda i: (i, 0, 0))],
        out_specs=pl.BlockSpec((step_rows, sub * lanes), lambda i: (i, 0)),
        cost_estimate=pl.CostEstimate(
            flops=0, transcendentals=0, bytes_accessed=4 * count * sub * lanes
        ),
        name="spread_rows",
    )(rows3)


def fold_kernel(rows_ref, out_ref):
    out_ref[...] = rows_ref[...].reshape(out_ref.shape)


def fold_rows(rows, step_rows=128):
    count, width = rows.shape
    lanes = width // SUB
    return pl.pallas_call(
        fold_kernel,
        out_shape=jax.ShapeDtypeStruct((count, SUB, lanes), jnp.bfloat16),
        grid=(count // step_rows,),
        in_specs=[pl.BlockSpec((step_rows, width), lambda i: (i, 0))],
        out_specs=pl.BlockSpec((step_rows, SUB, lanes), lambda i: (i, 0, 0)),
        cost_estimate=pl.CostEstimate(
            flops=0, transcendentals=0, bytes_accessed=4 * count * width
        ),
        name="fold_rows",
    )(rows)


VM = pl.BlockSpec(memory_space=pltpu.VMEM)
NT = (((1,), (1,)), ((), ()))
TN = (((0,), (0,)), ((), ()))


def turn(rows, cosines, sines):
    return rows * cosines + pltpu.roll(rows, rows.shape[1] // 2, 1) * sines


def unturn(rows, cosines, sines):
    return rows * cosines - pltpu.roll(rows, rows.shape[1] // 2, 1) * sines


def attend_kernel(
    normed_ref,
    query_w_ref,
    key_ref,
    value_ref,
    cos_ref,
    sin_ref,
    gain_ref,
    mask_ref,
    context_ref,
    raw_ref,
    weight_ref,
    held,
):
    step = pl.program_id(0)
    head_dim = key_ref.shape[1]
    heads = query_w_ref.shape[1] // head_dim

    @pl.when(step == 0)
    def _():
        held[...] = jnp.zeros_like(held)

    ready = held.at[lax.rem(step + 1, 2)]
    raw = ready[...]
    raw_ref[...] = raw
    held[lax.rem(step, 2)] = jnp.dot(
        normed_ref[...], query_w_ref[...], preferred_element_type=jnp.float32
    )
    factor = 1.0 / math.sqrt(head_dim)
    for g in range(heads):
        cols = slice(g * head_dim, (g + 1) * head_dim)
        own = raw[:, cols]
        scale = lax.rsqrt(jnp.sum(own * own, axis=1, keepdims=True) / head_dim + EPS)
        rows = turn(own * scale * gain_ref[...], cos_ref[...], sin_ref[...]).astype(jnp.bfloat16)
        scores = lax.dot_general(rows, key_ref[...], NT, preferred_element_type=jnp.float32)
        terms = jnp.exp(jnp.where(mask_ref[...] > 0.0, scores * factor, NEG))
        weights = terms / jnp.sum(terms, axis=1, keepdims=True)
        weight_ref[:, cols] = weights
        context = jnp.dot(
            weights.astype(jnp.bfloat16), value_ref[...], preferred_element_type=jnp.float32
        )
        context_ref[:, cols] = context.astype(jnp.bfloat16)


def attend(normed, query_w, key_rows, value_rows, cosines, sines, gain, mask, block=256):
    tokens, width = normed.shape
    columns = query_w.shape[1]
    steps = columns // block
    late = pl.BlockSpec((tokens, block), lambda i: (0, jnp.maximum(i - 1, 0)))
    whole = lambda a: pl.BlockSpec(a.shape, lambda i: (0, 0))
    return pl.pallas_call(
        attend_kernel,
        out_shape=(
            jax.ShapeDtypeStruct((tokens, columns), jnp.bfloat16),
            jax.ShapeDtypeStruct((tokens, columns), jnp.float32),
            jax.ShapeDtypeStruct((tokens, columns), jnp.float32),
        ),
        grid=(steps + 1,),
        in_specs=[
            whole(normed),
            pl.BlockSpec((width, block), lambda i: (0, jnp.minimum(i, steps - 1))),
            whole(key_rows),
            whole(value_rows),
            whole(cosines),
            whole(sines),
            whole(gain),
            whole(mask),
        ],
        out_specs=(late, late, late),
        scratch_shapes=[pltpu.VMEM((2, tokens, block), jnp.float32)],
        cost_estimate=pl.CostEstimate(
            flops=2 * tokens * width * columns,
            transcendentals=0,
            bytes_accessed=2 * width * columns,
        ),
        name="attend",
    )(normed, query_w, key_rows, value_rows, cosines, sines, gain, mask)


def attend_back_kernel(
    grad_ref,
    weight_ref,
    raw_ref,
    key_ref,
    value_ref,
    key_raw_ref,
    cos_ref,
    sin_ref,
    gain_ref,
    key_gain_ref,
    query_out,
    key_out,
    value_out,
    key_sum,
    value_sum,
):
    step = pl.program_id(0)
    head_dim = key_ref.shape[1]
    heads = grad_ref.shape[1] // head_dim
    factor = 1.0 / math.sqrt(head_dim)
    cosines, sines, gain = cos_ref[...], sin_ref[...], gain_ref[...]

    @pl.when(step == 0)
    def _():
        key_sum[...] = jnp.zeros_like(key_sum)
        value_sum[...] = jnp.zeros_like(value_sum)

    key_total, value_total = key_sum[...], value_sum[...]
    for g in range(heads):
        cols = slice(g * head_dim, (g + 1) * head_dim)
        grad = grad_ref[:, cols]
        weights = weight_ref[:, cols]
        own = raw_ref[:, cols]
        scale = lax.rsqrt(jnp.sum(own * own, axis=1, keepdims=True) / head_dim + EPS)
        rows = turn(own * scale * gain, cosines, sines).astype(jnp.bfloat16)
        grad_weights = lax.dot_general(grad, value_ref[...], NT, preferred_element_type=jnp.float32)
        value_total += lax.dot_general(
            weights.astype(jnp.bfloat16), grad, TN, preferred_element_type=jnp.float32
        )
        centered = grad_weights - jnp.sum(grad_weights * weights, axis=1, keepdims=True)
        grad_scores = (weights * centered * factor).astype(jnp.bfloat16)
        key_total += lax.dot_general(grad_scores, rows, TN, preferred_element_type=jnp.float32)
        grad_rows = jnp.dot(grad_scores, key_ref[...], preferred_element_type=jnp.float32)
        weighted = unturn(grad_rows, cosines, sines) * gain
        inner = jnp.sum(weighted * own, axis=1, keepdims=True) / head_dim
        query_out[:, cols] = (scale * weighted - own * (scale * scale * scale) * inner).astype(
            jnp.bfloat16
        )
    key_sum[...] = key_total
    value_sum[...] = value_total

    @pl.when(step == pl.num_programs(0) - 1)
    def _():
        own = key_raw_ref[...]
        scale = lax.rsqrt(jnp.sum(own * own, axis=1, keepdims=True) / head_dim + EPS)
        weighted = unturn(key_sum[...], cosines, sines) * key_gain_ref[...]
        inner = jnp.sum(weighted * own, axis=1, keepdims=True) / head_dim
        key_out[...] = (scale * weighted - own * (scale * scale * scale) * inner).astype(
            jnp.bfloat16
        )
        value_out[...] = value_sum[...].astype(jnp.bfloat16)


def attend_back(
    grad, weights, raw, key_rows, value_rows, key_raw, cosines, sines, gain, key_gain, block=512
):
    tokens, columns = grad.shape
    head_dim = key_rows.shape[1]
    piece = pl.BlockSpec((tokens, block), lambda i: (0, i))
    whole = lambda a: pl.BlockSpec(a.shape, lambda i: (0, 0))
    small = pl.BlockSpec((tokens, head_dim), lambda i: (0, 0))
    rest = (key_rows, value_rows, key_raw, cosines, sines, gain, key_gain)
    return pl.pallas_call(
        attend_back_kernel,
        out_shape=(
            jax.ShapeDtypeStruct((tokens, columns), jnp.bfloat16),
            jax.ShapeDtypeStruct((tokens, head_dim), jnp.bfloat16),
            jax.ShapeDtypeStruct((tokens, head_dim), jnp.bfloat16),
        ),
        grid=(columns // block,),
        in_specs=[piece, piece, piece, *map(whole, rest)],
        out_specs=(piece, small, small),
        scratch_shapes=[pltpu.VMEM((tokens, head_dim), jnp.float32)] * 2,
        cost_estimate=pl.CostEstimate(
            flops=12 * tokens * tokens * columns,
            transcendentals=0,
            bytes_accessed=12 * tokens * columns,
        ),
        name="attend_back",
    )(grad, weights, raw, *rest)


def project_kernel(at_ref, query_ref, key_ref, value_ref, query_w, key_w, value_w, out_ref):
    del at_ref
    total = lax.dot_general(query_ref[...], query_w[...], NT, preferred_element_type=jnp.float32)
    total += lax.dot_general(key_ref[...], key_w[...], NT, preferred_element_type=jnp.float32)
    total += lax.dot_general(value_ref[...], value_w[...], NT, preferred_element_type=jnp.float32)
    out_ref[...] = total.astype(out_ref.dtype)


def project_back(part, query_grad, key_grad, value_grad, query_w, key_w, value_w, dtype, block=512):
    tokens, columns = query_grad.shape
    width, _ = key_w.shape
    steps = width // 2 // block
    whole = lambda a: pl.BlockSpec(a.shape, lambda i, at: (0, 0))
    rows = lambda a: pl.BlockSpec((block, a.shape[1]), lambda i, at: (at[0] * steps + i, 0))
    return pl.pallas_call(
        project_kernel,
        out_shape=jax.ShapeDtypeStruct((tokens, width // 2), dtype),
        grid_spec=pltpu.PrefetchScalarGridSpec(
            num_scalar_prefetch=1,
            grid=(steps,),
            in_specs=[
                whole(query_grad),
                whole(key_grad),
                whole(value_grad),
                rows(query_w),
                rows(key_w),
                rows(value_w),
            ],
            out_specs=pl.BlockSpec((tokens, block), lambda i, at: (0, i)),
        ),
        cost_estimate=pl.CostEstimate(
            flops=tokens * columns * width,
            transcendentals=0,
            bytes_accessed=columns * width,
        ),
        name="project_back",
    )(part, query_grad, key_grad, value_grad, query_w, key_w, value_w)


def expert_kernel(
    rows_hbm,
    gate_hbm,
    up_hbm,
    cot_hbm,
    grad_hbm,
    hidden_ref,
    slot_ref,
    rows_v,
    gate_w,
    up_w,
    cot_ref,
    pre_gate,
    pre_up,
    grad_gate,
    grad_up,
    sem_in,
    sem_gate,
    sem_up,
    sem_cot,
    sem_out,
    *,
    chunks,
    row_block,
):
    count, sub, lanes = rows_v.shape
    width = sub * lanes
    piece, part = sub // chunks, width // chunks

    def arrive(k):
        at = pl.ds(k * piece, piece)
        return pltpu.make_async_copy(rows_hbm.at[:, at, :], rows_v.at[:, at, :], sem_in.at[k])

    def leave(k):
        at = pl.ds(k * piece, piece)
        return pltpu.make_async_copy(rows_v.at[:, at, :], grad_hbm.at[:, at, :], sem_out.at[k])

    def gate_in(k):
        at = pl.ds(k * part, part)
        return pltpu.make_async_copy(gate_hbm.at[at, :], gate_w.at[at, :], sem_gate.at[k])

    def up_in(k):
        at = pl.ds(k * part, part)
        return pltpu.make_async_copy(up_hbm.at[at, :], up_w.at[at, :], sem_up.at[k])

    cot_in = pltpu.make_async_copy(cot_hbm, cot_ref, sem_cot)
    for k in range(chunks):
        arrive(k).start()
        gate_in(k).start()
        up_in(k).start()
    cot_in.start()
    for k in range(chunks):
        arrive(k).wait()
        gate_in(k).wait()
        up_in(k).wait()
        rows = rows_v[:, k * piece : (k + 1) * piece, :].reshape(count, part)
        at = slice(k * part, (k + 1) * part)
        gate = jnp.dot(rows, gate_w[at, :], preferred_element_type=jnp.float32)
        up = jnp.dot(rows, up_w[at, :], preferred_element_type=jnp.float32)
        if k == 0:
            pre_gate[...] = gate
            pre_up[...] = up
        else:
            pre_gate[...] += gate
            pre_up[...] += up

    cot_in.wait()
    slot_count = slot_ref.shape[0]

    def between(r, carry):
        at = pl.ds(pl.multiple_of(r * row_block, 16), row_block)
        gate, up, cot = pre_gate[at, :], pre_up[at, :], cot_ref[at, :]
        sigmoid = 1.0 / (1.0 + jnp.exp(-gate))
        silu = gate * sigmoid
        hidden = (silu * up).astype(jnp.bfloat16)
        hidden_ref[at, :] = hidden
        grad_up[at, :] = (cot * silu).astype(jnp.bfloat16)
        grad_gate[at, :] = (cot * up * sigmoid * (1.0 + gate * (1.0 - sigmoid))).astype(
            jnp.bfloat16
        )
        slot = jnp.sum(hidden.astype(jnp.float32) * cot, axis=1, keepdims=True)
        row = lax.broadcasted_iota(jnp.int32, (row_block, 128), 0) + r * row_block
        block = jnp.floor((row.astype(jnp.float32) + 0.5) * (slot_count / count))
        block = block.astype(jnp.int32)
        lane = lax.broadcasted_iota(jnp.int32, (row_block, 128), 1)
        per = count // slot_count
        spread = jnp.where(row - block * per == lane, slot, 0.0)
        select = jnp.where(block == lane, 1.0, 0.0).astype(jnp.bfloat16)
        for _ in range(3):
            rounded = spread.astype(jnp.bfloat16)
            slot_ref[...] += lax.dot_general(
                select, rounded, TN, preferred_element_type=jnp.float32
            )
            spread = spread - rounded.astype(jnp.float32)
        return carry

    slot_ref[...] = jnp.zeros_like(slot_ref)

    lax.fori_loop(0, count // row_block, between, 0)
    for k in range(chunks):
        at = slice(k * part, (k + 1) * part)
        grad = lax.dot_general(grad_gate[...], gate_w[at, :], NT, preferred_element_type=jnp.float32)
        grad += lax.dot_general(grad_up[...], up_w[at, :], NT, preferred_element_type=jnp.float32)
        rows_v[:, k * piece : (k + 1) * piece, :] = grad.astype(jnp.bfloat16).reshape(
            count, piece, lanes
        )
        leave(k).start()
    for k in range(chunks):
        leave(k).wait()


def expert(rows3, gate_w, up_w, cot_hidden, slot_count, chunks=4, row_block=80):
    count = rows3.shape[0]
    inner = gate_w.shape[1]
    hbm = pl.BlockSpec(memory_space=pltpu.HBM)
    return pl.pallas_call(
        functools.partial(expert_kernel, chunks=chunks, row_block=row_block),
        out_shape=(
            jax.ShapeDtypeStruct(rows3.shape, jnp.bfloat16),
            jax.ShapeDtypeStruct((count, inner), jnp.bfloat16),
            jax.ShapeDtypeStruct((slot_count, 128), jnp.float32),
        ),
        in_specs=[hbm, hbm, hbm, hbm],
        out_specs=(hbm, VM, VM),
        scratch_shapes=[
            pltpu.VMEM(rows3.shape, jnp.bfloat16),
            pltpu.VMEM(gate_w.shape, jnp.bfloat16),
            pltpu.VMEM(up_w.shape, jnp.bfloat16),
            pltpu.VMEM((count, inner), jnp.float32),
            pltpu.VMEM((count, inner), jnp.float32),
            pltpu.VMEM((count, inner), jnp.float32),
            pltpu.VMEM((count, inner), jnp.bfloat16),
            pltpu.VMEM((count, inner), jnp.bfloat16),
            pltpu.SemaphoreType.DMA((chunks,)),
            pltpu.SemaphoreType.DMA((chunks,)),
            pltpu.SemaphoreType.DMA((chunks,)),
            pltpu.SemaphoreType.DMA,
            pltpu.SemaphoreType.DMA((chunks,)),
        ],
        compiler_params=pltpu.CompilerParams(vmem_limit_bytes=VMEM_LIMIT),
        cost_estimate=pl.CostEstimate(
            flops=8 * count * inner * gate_w.shape[0],
            transcendentals=0,
            bytes_accessed=4 * rows3.shape[0] * gate_w.shape[0],
        ),
        name="expert",
    )(rows3, gate_w, up_w, cot_hidden)


def swap_heads(values):
    return lax.ppermute(values, "head", [(0, 1), (1, 0)])


def exchange(rows3, device_count):
    count, sub, lanes = rows3.shape
    packed = rows3.reshape(device_count, (count // device_count) * sub, lanes)
    moved = lax.all_to_all(packed, ("req", "head"), split_axis=0, concat_axis=0, tiled=True)
    return moved.reshape(count, sub, lanes)


def device_step(
    layer_input,
    q_proj,
    key_proj,
    value_proj,
    query_gain,
    key_gain,
    attn_gain,
    moe_gain,
    router,
    expert_ids,
    req_lengths,
    w_gate,
    w_up,
    w_down,
    cotangent,
):
    head_count = lax.axis_size("head")
    head_index = lax.axis_index("head")
    device_count = lax.axis_size("req") * head_count
    token_count, width = layer_input.shape
    moe_tokens = token_count // head_count
    half_width = width // head_count
    capacity = 5
    first_core = head_index == 0

    query_w = lax.all_gather(q_proj, "req", axis=0, tiled=True)

    expert_range = jnp.arange(device_count, dtype=jnp.int32)
    chosen_mask = expert_ids[:, :, None] == expert_range[None, None, :]
    member = jnp.any(chosen_mask, axis=1)
    token_range = jnp.arange(moe_tokens, dtype=jnp.int32)
    before = (token_range[:, None] > token_range[None, :]).astype(jnp.bfloat16)
    rank = jnp.dot(before, member.astype(jnp.bfloat16), preferred_element_type=jnp.float32)
    rank = rank.astype(jnp.int32)
    slot_of = jnp.sum(jnp.where(chosen_mask, rank[:, None, :], 0), axis=2)
    target = (expert_ids * capacity + slot_of).reshape(-1)
    slot_range = jnp.arange(capacity, dtype=jnp.int32)
    hit = member[:, :, None] & (rank[:, :, None] == slot_range[None, None, :])
    source = jnp.sum(jnp.where(hit, token_range[:, None, None], 0), axis=0).reshape(-1)

    cot_send = pick_rows(cotangent, source)

    segment, offsets = segments_of(req_lengths[0], token_count)
    input32 = layer_input.astype(jnp.float32)
    input_scale = rms_scale(input32)
    normed = (input32 * input_scale * attn_gain[None, :]).astype(jnp.bfloat16)
    head_dim = key_proj.shape[1]
    cosine_table, sine_table = rope_tables(offsets, head_dim // 2)
    key_raw = jnp.dot(normed, key_proj, preferred_element_type=jnp.float32)
    key_normed = key_raw * rms_scale(key_raw) * key_gain
    key_rows = rotate(key_normed, cosine_table, sine_table).astype(jnp.bfloat16)
    value_rows = jnp.dot(normed, value_proj, preferred_element_type=jnp.float32)
    value_rows = value_rows.astype(jnp.bfloat16)
    places = jnp.arange(token_count, dtype=jnp.int32)
    allowed = (segment[:, None] == segment[None, :]) & (places[None, :] <= places[:, None])
    mask = allowed.astype(jnp.float32)
    cosines = jnp.concatenate([cosine_table, cosine_table], axis=1)
    sines = jnp.concatenate([-sine_table, sine_table], axis=1)
    query_gain2, key_gain2 = query_gain[None, :], key_gain[None, :]
    prep = (cot_send, query_w, normed, key_raw, key_rows, value_rows, cosines, sines, mask)
    prep = (*prep, target)
    prep = lax.optimization_barrier(prep)
    cot_send, query_w, normed, key_raw, key_rows, value_rows, cosines, sines, mask, target = prep
    cot_rows3 = exchange(cot_send, device_count)
    context, query_raw, attn_weights = attend(
        normed, query_w, key_rows, value_rows, cosines, sines, query_gain2, mask
    )
    other_rows = lax.dynamic_slice_in_dim(context, (1 - head_index) * moe_tokens, moe_tokens, 0)
    own_rows = lax.dynamic_slice_in_dim(context, head_index * moe_tokens, moe_tokens, 0)
    came = swap_heads(other_rows)
    context_tok = jnp.concatenate(
        [jnp.where(first_core, own_rows, came), jnp.where(first_core, came, own_rows)], axis=1
    )
    own_input = lax.dynamic_slice_in_dim(layer_input, head_index * moe_tokens, moe_tokens, 0)
    residual = own_input.astype(jnp.float32) + context_tok.astype(jnp.float32)
    moe_scale = rms_scale(residual)
    moe_in = (residual * moe_scale * moe_gain[None, :]).astype(jnp.bfloat16)
    moe_send = pick_rows(moe_in, source)
    rows3 = exchange(moe_send, device_count)

    logits = jnp.dot(moe_in, router, preferred_element_type=jnp.float32)
    chosen = jnp.sum(jnp.where(chosen_mask, logits[:, None, :], 0.0), axis=2)
    gates = jax.nn.softmax(chosen, axis=1)
    flat_gates = gates.reshape(-1)
    cot32 = cotangent.astype(jnp.float32)

    gate_w = w_gate[0]
    up_w = w_up[0]
    down_w = w_down[0]
    cot_rows = spread_rows(cot_rows3)
    cot_hidden = jnp.dot(cot_rows, down_w.T, preferred_element_type=jnp.float32)
    cot_hidden = lax.optimization_barrier(cot_hidden)
    grad_send, hidden, slot_grad = expert(rows3, gate_w, up_w, cot_hidden, device_count)
    slot_back = lax.all_to_all(
        slot_grad.reshape(device_count, 1, 128),
        ("req", "head"),
        split_axis=0,
        concat_axis=0,
        tiled=True,
    )
    slot_back = slot_back.reshape(device_count, 128)[:, :capacity]
    grad_back = exchange(grad_send, device_count)
    outputs = jnp.dot(hidden, down_w, preferred_element_type=jnp.float32).astype(jnp.bfloat16)
    out_send = fold_rows(outputs)
    out_back = exchange(out_send, device_count)

    hit_grad = jnp.sum(jnp.where(hit, slot_back[None, :, :], 0.0), axis=2)
    gate_grad = jnp.sum(jnp.where(chosen_mask, hit_grad[:, None, :], 0.0), axis=2)
    total_gate = jnp.sum(gates * gate_grad, axis=1, keepdims=True)
    grad_logit = gates * (gate_grad - total_gate)
    dense = jnp.sum(jnp.where(chosen_mask, grad_logit[:, :, None], 0.0), axis=1)
    router_part = jnp.dot(
        dense, router.astype(jnp.float32).T, precision=lax.Precision.HIGHEST
    )
    router_part = lax.optimization_barrier(router_part)
    grad_in = mix_rows(grad_back, target, flat_gates, moe_tokens, router_part[:8, :128])
    grad_in = grad_in.reshape(moe_tokens, width)
    grad_in = grad_in + router_part
    grad_resid = cot32 + norm_backward(residual, moe_scale, moe_gain, grad_in)
    left, right = grad_resid[:, :half_width], grad_resid[:, half_width:]
    came_grad = swap_heads(jnp.where(first_core, right, left))
    own_grad = jnp.where(first_core, left, right)
    grad_heads = jnp.concatenate(
        [jnp.where(first_core, own_grad, came_grad), jnp.where(first_core, came_grad, own_grad)],
        axis=0,
    )
    query_grad, key_grad, value_grad = attend_back(
        grad_heads.astype(jnp.bfloat16),
        attn_weights,
        query_raw,
        key_rows,
        value_rows,
        key_raw,
        cosines,
        sines,
        query_gain2,
        key_gain2,
    )
    weights3 = (query_w, key_proj, value_proj)
    grads3 = (query_grad, key_grad, value_grad)
    other_half = project_back((1 - head_index)[None], *grads3, *weights3, jnp.bfloat16)
    came_half = swap_heads(other_half)
    own_half = project_back(head_index[None], *grads3, *weights3, jnp.float32)
    input_half = lax.dynamic_slice_in_dim(layer_input, head_index * half_width, half_width, 1)
    input_half = input_half.astype(jnp.float32)
    gain_half = lax.dynamic_slice_in_dim(attn_gain, head_index * half_width, half_width, 0)
    weighted = (own_half + came_half.astype(jnp.float32)) * gain_half[None, :]
    inner_part = jnp.sum(weighted * input_half, axis=1)
    direct_part = jnp.sum(grad_heads * input_half, axis=1)
    parts = jnp.stack([inner_part, direct_part], axis=0)
    inner_sum, direct_sum = parts + swap_heads(parts)
    inner = inner_sum[:, None] / width
    grad_attn = input_scale * weighted - input_half * input_scale**3 * inner
    attribution = (grad_heads + grad_attn) * input_half
    square_sum = jnp.sum(input32 * input32, axis=1)
    scale_row = input_scale[:, 0]
    token_score = direct_sum + (
        scale_row * inner_sum - scale_row**3 * (inner_sum / width) * square_sum
    )
    moe_sum = mix_rows(out_back, target, flat_gates, moe_tokens, own_half[:8, :128]).reshape(moe_tokens, width)
    mixed = (residual + moe_sum).astype(jnp.bfloat16)
    return (mixed, attribution, token_score)


def solution(mesh):
    return jax.shard_map(
        device_step,
        mesh=mesh,
        in_specs=(
            P("req", None),
            P("req", "head"),
            P(None, "head"),
            P(None, "head"),
            P(),
            P(),
            P(),
            P(),
            P(),
            P(("req", "head"), None),
            P("req", None),
            P(("req", "head"), None, None),
            P(("req", "head"), None, None),
            P(("req", "head"), None, None),
            P(("req", "head"), None),
        ),
        out_specs=(P(("req", "head"), None), P("req", "head"), P("req")),
        check_vma=False,
    )
```

```python
import functools
import math

import jax
import jax.numpy as jnp
from jax import lax
from jax.experimental import pallas as pl
from jax.experimental.pallas import tpu as pltpu
from jax.sharding import PartitionSpec as P


EPS = 1e-06
THETA = 1000000.0
NEG = -1e30


def segments_of(lengths_row, token_count):
    ends = jnp.cumsum(lengths_row)
    starts = ends - lengths_row
    places = jnp.arange(token_count, dtype=jnp.int32)
    segment = jnp.sum((places[:, None] >= ends[None, :]).astype(jnp.int32), axis=1)
    picked = (
        segment[:, None] == jnp.arange(lengths_row.shape[0], dtype=jnp.int32)[None, :]
    ).astype(jnp.int32)
    start_of = jnp.sum(picked * starts[None, :], axis=1)
    return (segment, places - start_of)


def rope_tables(offsets, half_dim):
    freq = THETA ** (-jnp.arange(half_dim, dtype=jnp.float32) / half_dim)
    angle = offsets.astype(jnp.float32)[:, None] * freq[None, :]
    return (jnp.cos(angle), jnp.sin(angle))


def rotate(rows, cosine_table, sine_table):
    half_dim = rows.shape[-1] // 2
    first = rows[..., :half_dim]
    second = rows[..., half_dim:]
    return jnp.concatenate(
        [first * cosine_table - second * sine_table, second * cosine_table + first * sine_table],
        axis=-1,
    )


def rms_scale(values):
    return lax.rsqrt(jnp.mean(values * values, axis=-1, keepdims=True) + EPS)


def norm_backward(values, scale, gain, grad_out):
    weighted = grad_out * gain
    inner = jnp.mean(weighted * values, axis=-1, keepdims=True)
    return scale * weighted - values * scale**3 * inner


SUB = 32
PART = 1024
VMEM_LIMIT = 56 * 1024 * 1024


def pick_kernel(index_ref, rows_ref, out_ref, folded):
    step_rows = out_ref.shape[0]
    base = pl.program_id(0) * step_rows

    @pl.when(pl.program_id(0) == 0)
    def _():
        folded[...] = rows_ref[...].reshape(folded.shape)

    def one(i, carry):
        out_ref[i] = folded[index_ref[base + i]]
        return carry

    lax.fori_loop(0, step_rows, one, 0, unroll=8)


def pick_rows(rows, index, step_rows=80):
    count = index.shape[0]
    tokens, width = rows.shape
    lanes = width // SUB
    return pl.pallas_call(
        pick_kernel,
        out_shape=jax.ShapeDtypeStruct((count, SUB, lanes), rows.dtype),
        grid_spec=pltpu.PrefetchScalarGridSpec(
            num_scalar_prefetch=1,
            grid=(count // step_rows,),
            in_specs=[pl.BlockSpec(rows.shape, lambda i, ids: (0, 0))],
            out_specs=pl.BlockSpec((step_rows, SUB, lanes), lambda i, ids: (i, 0, 0)),
            scratch_shapes=[pltpu.VMEM((tokens, SUB, lanes), rows.dtype)],
        ),
        cost_estimate=pl.CostEstimate(
            flops=0, transcendentals=0, bytes_accessed=count * width * 2
        ),
        name="pick_rows",
    )(index, rows)


def mix_block(id_ref, slot_ref, gate_ref, rows_ref, total):
    tokens = total.shape[0]
    top = id_ref.shape[0] // tokens

    def one(i, carry):
        at = i * top
        row = gate_ref[at] * rows_ref[id_ref[at], slot_ref[at]].astype(jnp.float32)
        for k in range(1, top):
            own = rows_ref[id_ref[at + k], slot_ref[at + k]].astype(jnp.float32)
            row = row + gate_ref[at + k] * own
        total[i] = row
        return carry

    lax.fori_loop(0, tokens, one, 0, unroll=4)


def mix_out_kernel(id_ref, slot_ref, gate_ref, rows_ref, base_ref, after_ref, out_ref, total):
    del after_ref
    mix_block(id_ref, slot_ref, gate_ref, rows_ref, total)
    mixed = base_ref[...] + total[...].reshape(out_ref.shape)
    out_ref[...] = mixed.astype(out_ref.dtype)


def mix_grad_kernel(id_ref, slot_ref, gate_ref, rows_ref, extra_ref, after_ref, out_ref, sum_ref, total):
    del after_ref
    mix_block(id_ref, slot_ref, gate_ref, rows_ref, total)
    out_ref[...] = total[...].reshape(out_ref.shape)
    tokens = total.shape[0]
    top = id_ref.shape[0] // tokens

    @pl.when(pl.program_id(0) == 0)
    def _():
        line = lax.broadcasted_iota(jnp.int32, extra_ref.shape[2:], 0)

        def one(i, carry):
            tile = jnp.zeros(extra_ref.shape[2:], jnp.float32)
            for k in range(top):
                at = i * top + k
                own = gate_ref[at] * extra_ref[id_ref[at], 0].astype(jnp.float32)
                tile = tile + jnp.where(line == slot_ref[at], own, 0.0)
            sum_ref[pl.ds(i, 1), :] = jnp.sum(tile, axis=0, keepdims=True)
            return carry

        lax.fori_loop(0, tokens, one, 0, unroll=2)


def mix_rows(back4, ids, places, gates, base, after, capacity):
    blocks, _, sub, lanes = back4.shape
    top_tokens = ids.shape[0]
    tokens = after.shape[0]
    part = sub * lanes
    steps = SUB // sub
    rows_spec = pl.BlockSpec((blocks, capacity, sub, lanes), lambda k, *_: (0, k, 0, 0))
    wide = pl.BlockSpec((tokens, part), lambda k, *_: (0, k))
    flat = pl.BlockSpec((tokens, lanes), lambda k, *_: (0, 0))
    if base is None:
        extra = pl.BlockSpec((blocks, 1, sub, lanes), lambda k, *_: (0, steps * capacity, 0, 0))
        kernel, specs, operands = mix_grad_kernel, [rows_spec, extra, flat], (back4, back4, after)
        out_shape = (
            jax.ShapeDtypeStruct((tokens, steps * part), jnp.float32),
            jax.ShapeDtypeStruct((tokens, lanes), jnp.float32),
        )
        out_specs = (wide, flat)
    else:
        kernel, specs, operands = mix_out_kernel, [rows_spec, wide, flat], (back4, base, after)
        out_shape = jax.ShapeDtypeStruct((tokens, steps * part), jnp.bfloat16)
        out_specs = wide
    return pl.pallas_call(
        kernel,
        out_shape=out_shape,
        grid_spec=pltpu.PrefetchScalarGridSpec(
            num_scalar_prefetch=3,
            grid=(steps,),
            in_specs=specs,
            out_specs=out_specs,
            scratch_shapes=[pltpu.VMEM((tokens, sub, lanes), jnp.float32)],
        ),
        cost_estimate=pl.CostEstimate(
            flops=top_tokens * steps * part * 2,
            transcendentals=0,
            bytes_accessed=blocks * capacity * steps * part * 2,
        ),
        name="mix_rows",
    )(ids, places, gates, *operands)


def spread_kernel(rows_ref, out_ref):
    out_ref[...] = rows_ref[...].reshape(out_ref.shape)


def spread_rows(rows3, step_rows=128):
    count, sub, lanes = rows3.shape
    return pl.pallas_call(
        spread_kernel,
        out_shape=jax.ShapeDtypeStruct((count, sub * lanes), rows3.dtype),
        grid=(count // step_rows,),
        in_specs=[pl.BlockSpec((step_rows, sub, lanes), lambda i: (i, 0, 0))],
        out_specs=pl.BlockSpec((step_rows, sub * lanes), lambda i: (i, 0)),
        cost_estimate=pl.CostEstimate(
            flops=0, transcendentals=0, bytes_accessed=4 * count * sub * lanes
        ),
        name="spread_rows",
    )(rows3)


def fold_kernel(rows_ref, out_ref):
    blocks, places, sub, lanes = out_ref.shape
    part = sub * lanes
    parts = rows_ref.shape[1] // part
    per = places // parts
    for k in range(parts):
        rows = rows_ref[:, k * part : (k + 1) * part]
        out_ref[:, k * per : (k + 1) * per] = rows.reshape(blocks, per, sub, lanes)


def fold_rows(rows, capacity, step_blocks=32):
    count, width = rows.shape
    blocks = count // capacity
    places = capacity * width // PART
    return pl.pallas_call(
        fold_kernel,
        out_shape=jax.ShapeDtypeStruct((blocks, places, 8, PART // 8), jnp.bfloat16),
        grid=(blocks // step_blocks,),
        in_specs=[pl.BlockSpec((step_blocks * capacity, width), lambda i: (i, 0))],
        out_specs=pl.BlockSpec((step_blocks, places, 8, PART // 8), lambda i: (i, 0, 0, 0)),
        cost_estimate=pl.CostEstimate(
            flops=0, transcendentals=0, bytes_accessed=4 * count * width
        ),
        name="fold_rows",
    )(rows)


VM = pl.BlockSpec(memory_space=pltpu.VMEM)
NT = (((1,), (1,)), ((), ()))
TN = (((0,), (0,)), ((), ()))


def turn(rows, cosines, sines):
    return rows * cosines + pltpu.roll(rows, rows.shape[1] // 2, 1) * sines


def unturn(rows, cosines, sines):
    return rows * cosines - pltpu.roll(rows, rows.shape[1] // 2, 1) * sines


def attend_kernel(
    normed_ref,
    query_w_ref,
    key_ref,
    value_ref,
    cos_ref,
    sin_ref,
    gain_ref,
    mask_ref,
    context_ref,
    raw_ref,
    weight_ref,
    held,
):
    step = pl.program_id(0)
    head_dim = key_ref.shape[1]
    heads = query_w_ref.shape[1] // head_dim

    @pl.when(step == 0)
    def _():
        held[...] = jnp.zeros_like(held)

    ready = held.at[lax.rem(step + 1, 2)]
    raw = ready[...]
    raw_ref[...] = raw
    held[lax.rem(step, 2)] = jnp.dot(
        normed_ref[...], query_w_ref[...], preferred_element_type=jnp.float32
    )
    factor = 1.0 / math.sqrt(head_dim)
    for g in range(heads):
        cols = slice(g * head_dim, (g + 1) * head_dim)
        own = raw[:, cols]
        scale = lax.rsqrt(jnp.sum(own * own, axis=1, keepdims=True) / head_dim + EPS)
        rows = turn(own * scale * gain_ref[...], cos_ref[...], sin_ref[...]).astype(jnp.bfloat16)
        scores = lax.dot_general(rows, key_ref[...], NT, preferred_element_type=jnp.float32)
        terms = jnp.exp(jnp.where(mask_ref[...] > 0.0, scores * factor, NEG))
        weights = terms / jnp.sum(terms, axis=1, keepdims=True)
        weight_ref[:, cols] = weights
        context = jnp.dot(
            weights.astype(jnp.bfloat16), value_ref[...], preferred_element_type=jnp.float32
        )
        context_ref[:, cols] = context.astype(jnp.bfloat16)


def attend(normed, query_w, key_rows, value_rows, cosines, sines, gain, mask, block=256):
    tokens, width = normed.shape
    columns = query_w.shape[1]
    steps = columns // block
    late = pl.BlockSpec((tokens, block), lambda i: (0, jnp.maximum(i - 1, 0)))
    whole = lambda a: pl.BlockSpec(a.shape, lambda i: (0, 0))
    return pl.pallas_call(
        attend_kernel,
        out_shape=(
            jax.ShapeDtypeStruct((tokens, columns), jnp.bfloat16),
            jax.ShapeDtypeStruct((tokens, columns), jnp.float32),
            jax.ShapeDtypeStruct((tokens, columns), jnp.float32),
        ),
        grid=(steps + 1,),
        in_specs=[
            whole(normed),
            pl.BlockSpec((width, block), lambda i: (0, jnp.minimum(i, steps - 1))),
            whole(key_rows),
            whole(value_rows),
            whole(cosines),
            whole(sines),
            whole(gain),
            whole(mask),
        ],
        out_specs=(late, late, late),
        scratch_shapes=[pltpu.VMEM((2, tokens, block), jnp.float32)],
        cost_estimate=pl.CostEstimate(
            flops=2 * tokens * width * columns,
            transcendentals=0,
            bytes_accessed=2 * width * columns,
        ),
        name="attend",
    )(normed, query_w, key_rows, value_rows, cosines, sines, gain, mask)


def attend_back_kernel(
    grad_ref,
    weight_ref,
    raw_ref,
    key_ref,
    value_ref,
    key_raw_ref,
    cos_ref,
    sin_ref,
    gain_ref,
    key_gain_ref,
    query_out,
    key_out,
    value_out,
    key_sum,
    value_sum,
):
    step = pl.program_id(0)
    head_dim = key_ref.shape[1]
    heads = grad_ref.shape[1] // head_dim
    factor = 1.0 / math.sqrt(head_dim)
    cosines, sines, gain = cos_ref[...], sin_ref[...], gain_ref[...]

    @pl.when(step == 0)
    def _():
        key_sum[...] = jnp.zeros_like(key_sum)
        value_sum[...] = jnp.zeros_like(value_sum)

    key_total, value_total = key_sum[...], value_sum[...]
    for g in range(heads):
        cols = slice(g * head_dim, (g + 1) * head_dim)
        grad = grad_ref[:, cols]
        weights = weight_ref[:, cols]
        own = raw_ref[:, cols]
        scale = lax.rsqrt(jnp.sum(own * own, axis=1, keepdims=True) / head_dim + EPS)
        rows = turn(own * scale * gain, cosines, sines).astype(jnp.bfloat16)
        grad_weights = lax.dot_general(grad, value_ref[...], NT, preferred_element_type=jnp.float32)
        value_total += lax.dot_general(
            weights.astype(jnp.bfloat16), grad, TN, preferred_element_type=jnp.float32
        )
        centered = grad_weights - jnp.sum(grad_weights * weights, axis=1, keepdims=True)
        grad_scores = (weights * centered * factor).astype(jnp.bfloat16)
        key_total += lax.dot_general(grad_scores, rows, TN, preferred_element_type=jnp.float32)
        grad_rows = jnp.dot(grad_scores, key_ref[...], preferred_element_type=jnp.float32)
        weighted = unturn(grad_rows, cosines, sines) * gain
        inner = jnp.sum(weighted * own, axis=1, keepdims=True) / head_dim
        query_out[:, cols] = (scale * weighted - own * (scale * scale * scale) * inner).astype(
            jnp.bfloat16
        )
    key_sum[...] = key_total
    value_sum[...] = value_total

    @pl.when(step == pl.num_programs(0) - 1)
    def _():
        own = key_raw_ref[...]
        scale = lax.rsqrt(jnp.sum(own * own, axis=1, keepdims=True) / head_dim + EPS)
        weighted = unturn(key_sum[...], cosines, sines) * key_gain_ref[...]
        inner = jnp.sum(weighted * own, axis=1, keepdims=True) / head_dim
        key_out[...] = (scale * weighted - own * (scale * scale * scale) * inner).astype(
            jnp.bfloat16
        )
        value_out[...] = value_sum[...].astype(jnp.bfloat16)


def attend_back(
    grad, weights, raw, key_rows, value_rows, key_raw, cosines, sines, gain, key_gain, block=512
):
    tokens, columns = grad.shape
    head_dim = key_rows.shape[1]
    piece = pl.BlockSpec((tokens, block), lambda i: (0, i))
    whole = lambda a: pl.BlockSpec(a.shape, lambda i: (0, 0))
    small = pl.BlockSpec((tokens, head_dim), lambda i: (0, 0))
    rest = (key_rows, value_rows, key_raw, cosines, sines, gain, key_gain)
    return pl.pallas_call(
        attend_back_kernel,
        out_shape=(
            jax.ShapeDtypeStruct((tokens, columns), jnp.bfloat16),
            jax.ShapeDtypeStruct((tokens, head_dim), jnp.bfloat16),
            jax.ShapeDtypeStruct((tokens, head_dim), jnp.bfloat16),
        ),
        grid=(columns // block,),
        in_specs=[piece, piece, piece, *map(whole, rest)],
        out_specs=(piece, small, small),
        scratch_shapes=[pltpu.VMEM((tokens, head_dim), jnp.float32)] * 2,
        cost_estimate=pl.CostEstimate(
            flops=12 * tokens * tokens * columns,
            transcendentals=0,
            bytes_accessed=12 * tokens * columns,
        ),
        name="attend_back",
    )(grad, weights, raw, *rest)


def project_kernel(at_ref, query_ref, key_ref, value_ref, query_w, key_w, value_w, out_ref):
    del at_ref
    total = lax.dot_general(query_ref[...], query_w[...], NT, preferred_element_type=jnp.float32)
    total += lax.dot_general(key_ref[...], key_w[...], NT, preferred_element_type=jnp.float32)
    total += lax.dot_general(value_ref[...], value_w[...], NT, preferred_element_type=jnp.float32)
    out_ref[...] = total.astype(out_ref.dtype)


def project_back(part, query_grad, key_grad, value_grad, query_w, key_w, value_w, dtype, block=512):
    tokens, columns = query_grad.shape
    width, _ = key_w.shape
    steps = width // 2 // block
    whole = lambda a: pl.BlockSpec(a.shape, lambda i, at: (0, 0))
    rows = lambda a: pl.BlockSpec((block, a.shape[1]), lambda i, at: (at[0] * steps + i, 0))
    return pl.pallas_call(
        project_kernel,
        out_shape=jax.ShapeDtypeStruct((tokens, width // 2), dtype),
        grid_spec=pltpu.PrefetchScalarGridSpec(
            num_scalar_prefetch=1,
            grid=(steps,),
            in_specs=[
                whole(query_grad),
                whole(key_grad),
                whole(value_grad),
                rows(query_w),
                rows(key_w),
                rows(value_w),
            ],
            out_specs=pl.BlockSpec((tokens, block), lambda i, at: (0, i)),
        ),
        cost_estimate=pl.CostEstimate(
            flops=tokens * columns * width,
            transcendentals=0,
            bytes_accessed=columns * width,
        ),
        name="project_back",
    )(part, query_grad, key_grad, value_grad, query_w, key_w, value_w)


def expert_kernel(
    rows_hbm,
    gate_hbm,
    up_hbm,
    cot_hbm,
    router_ref,
    grad_hbm,
    hidden_ref,
    rows_v,
    made_v,
    slot_v,
    gate_w,
    up_w,
    cot_ref,
    pre_gate,
    pre_up,
    grad_gate,
    grad_up,
    sem_in,
    sem_gate,
    sem_up,
    sem_cot,
    sem_out,
    *,
    chunks,
    row_block,
):
    count, sub, lanes = rows_v.shape
    width = sub * lanes
    piece, part = sub // chunks, width // chunks

    def arrive(k):
        at = pl.ds(k * piece, piece)
        return pltpu.make_async_copy(rows_hbm.at[:, at, :], rows_v.at[:, at, :], sem_in.at[k])

    blocks, places = made_v.shape[:2]
    per = count // blocks

    def leave(k):
        at = pl.ds(k * per, per if k < chunks else places - chunks * per)
        return pltpu.make_async_copy(made_v.at[:, at], grad_hbm.at[:, at], sem_out.at[k])

    def gate_in(k):
        at = pl.ds(k * part, part)
        return pltpu.make_async_copy(gate_hbm.at[at, :], gate_w.at[at, :], sem_gate.at[k])

    def up_in(k):
        at = pl.ds(k * part, part)
        return pltpu.make_async_copy(up_hbm.at[at, :], up_w.at[at, :], sem_up.at[k])

    cot_in = pltpu.make_async_copy(cot_hbm, cot_ref, sem_cot)
    for k in range(chunks):
        arrive(k).start()
        gate_in(k).start()
        up_in(k).start()
    cot_in.start()
    for k in range(chunks):
        arrive(k).wait()
        gate_in(k).wait()
        up_in(k).wait()
        rows = rows_v[:, k * piece : (k + 1) * piece, :].reshape(count, part)
        at = slice(k * part, (k + 1) * part)
        gate = jnp.dot(rows, gate_w[at, :], preferred_element_type=jnp.float32)
        up = jnp.dot(rows, up_w[at, :], preferred_element_type=jnp.float32)
        if k == 0:
            pre_gate[...] = gate
            pre_up[...] = up
        else:
            pre_gate[...] += gate
            pre_up[...] += up

    cot_in.wait()

    def between(r, carry):
        at = pl.ds(pl.multiple_of(r * row_block, 16), row_block)
        gate, up, cot = pre_gate[at, :], pre_up[at, :], cot_ref[at, :]
        sigmoid = 1.0 / (1.0 + jnp.exp(-gate))
        silu = gate * sigmoid
        hidden = (silu * up).astype(jnp.bfloat16)
        hidden_ref[at, :] = hidden
        grad_up[at, :] = (cot * silu).astype(jnp.bfloat16)
        grad_gate[at, :] = (cot * up * sigmoid * (1.0 + gate * (1.0 - sigmoid))).astype(
            jnp.bfloat16
        )
        slot = jnp.sum(hidden.astype(jnp.float32) * cot, axis=1, keepdims=True)
        slot_v[at, :] = jnp.broadcast_to(slot, (row_block, slot_v.shape[1]))
        return carry

    lax.fori_loop(0, count // row_block, between, 0)
    for k in range(chunks):
        at = slice(k * part, (k + 1) * part)
        grad = lax.dot_general(grad_gate[...], gate_w[at, :], NT, preferred_element_type=jnp.float32)
        grad += lax.dot_general(grad_up[...], up_w[at, :], NT, preferred_element_type=jnp.float32)
        grad += slot_v[:, :1] * router_ref[:, at]
        made_v[:, k * per : (k + 1) * per] = grad.astype(jnp.bfloat16).reshape(
            blocks, per, piece, lanes
        )
        leave(k).start()
    slot = slot_v[...]
    upper = slot.astype(jnp.bfloat16)
    lower = (slot - upper.astype(jnp.float32)).astype(jnp.bfloat16)
    lane = lax.broadcasted_iota(jnp.int32, slot.shape, 1)
    value = jnp.where(lane < lanes // 2, upper.astype(jnp.float32), lower.astype(jnp.float32))
    value = value.astype(jnp.bfloat16)
    group = 16
    column = lax.broadcasted_iota(jnp.int32, (group * 8, count), 1)
    line = lax.broadcasted_iota(jnp.int32, (group * 8, count), 0)
    for b in range(0, blocks, group):
        block, place = lax.shift_right_logical(line, 3) + b, line & 7
        select = jnp.where((block * per + place == column) & (place < per), 1.0, 0.0)
        extra = jnp.dot(select.astype(jnp.bfloat16), value, preferred_element_type=jnp.float32)
        made_v[b : b + group, chunks * per] = extra.astype(jnp.bfloat16).reshape(group, 8, lanes)
    leave(chunks).start()
    for k in range(chunks + 1):
        leave(k).wait()


def expert(rows3, gate_w, up_w, cot_hidden, router_row, blocks, chunks=4, row_block=80):
    count, sub, lanes = rows3.shape
    made = (blocks, chunks * count // blocks + 1, sub // chunks, lanes)
    inner = gate_w.shape[1]
    hbm = pl.BlockSpec(memory_space=pltpu.HBM)
    return pl.pallas_call(
        functools.partial(expert_kernel, chunks=chunks, row_block=row_block),
        out_shape=(
            jax.ShapeDtypeStruct(made, jnp.bfloat16),
            jax.ShapeDtypeStruct((count, inner), jnp.bfloat16),
        ),
        in_specs=[hbm, hbm, hbm, hbm, VM],
        out_specs=(hbm, VM),
        scratch_shapes=[
            pltpu.VMEM(rows3.shape, jnp.bfloat16),
            pltpu.VMEM(made, jnp.bfloat16),
            pltpu.VMEM((count, lanes), jnp.float32),
            pltpu.VMEM(gate_w.shape, jnp.bfloat16),
            pltpu.VMEM(up_w.shape, jnp.bfloat16),
            pltpu.VMEM((count, inner), jnp.float32),
            pltpu.VMEM((count, inner), jnp.float32),
            pltpu.VMEM((count, inner), jnp.float32),
            pltpu.VMEM((count, inner), jnp.bfloat16),
            pltpu.VMEM((count, inner), jnp.bfloat16),
            pltpu.SemaphoreType.DMA((chunks,)),
            pltpu.SemaphoreType.DMA((chunks,)),
            pltpu.SemaphoreType.DMA((chunks,)),
            pltpu.SemaphoreType.DMA,
            pltpu.SemaphoreType.DMA((chunks + 1,)),
        ],
        compiler_params=pltpu.CompilerParams(vmem_limit_bytes=VMEM_LIMIT),
        cost_estimate=pl.CostEstimate(
            flops=8 * count * inner * gate_w.shape[0],
            transcendentals=0,
            bytes_accessed=4 * rows3.shape[0] * gate_w.shape[0],
        ),
        name="expert",
    )(rows3, gate_w, up_w, cot_hidden, router_row)


def swap_heads(values):
    return lax.ppermute(values, "head", [(0, 1), (1, 0)])


def exchange(rows, device_count):
    packed = rows.reshape(device_count, -1, 128)
    moved = lax.all_to_all(packed, ("req", "head"), split_axis=0, concat_axis=0, tiled=True)
    return moved.reshape(rows.shape)


def device_step(
    layer_input,
    q_proj,
    key_proj,
    value_proj,
    query_gain,
    key_gain,
    attn_gain,
    moe_gain,
    router,
    expert_ids,
    req_lengths,
    w_gate,
    w_up,
    w_down,
    cotangent,
):
    head_count = lax.axis_size("head")
    head_index = lax.axis_index("head")
    device_count = lax.axis_size("req") * head_count
    token_count, width = layer_input.shape
    moe_tokens = token_count // head_count
    half_width = width // head_count
    capacity = 5
    first_core = head_index == 0

    query_w = lax.all_gather(q_proj, "req", axis=0, tiled=True)

    expert_range = jnp.arange(device_count, dtype=jnp.int32)
    chosen_mask = expert_ids[:, :, None] == expert_range[None, None, :]
    member = jnp.any(chosen_mask, axis=1)
    token_range = jnp.arange(moe_tokens, dtype=jnp.int32)
    before = (token_range[:, None] > token_range[None, :]).astype(jnp.bfloat16)
    rank = jnp.dot(before, member.astype(jnp.bfloat16), preferred_element_type=jnp.float32)
    rank = rank.astype(jnp.int32)
    slot_of = jnp.sum(jnp.where(chosen_mask, rank[:, None, :], 0), axis=2)
    flat_ids, flat_slots = expert_ids.reshape(-1), slot_of.reshape(-1)
    device_index = lax.axis_index("req") * head_count + head_index
    router_row = lax.dynamic_slice_in_dim(router, device_index, 1, 1).astype(jnp.float32).T
    slot_range = jnp.arange(capacity, dtype=jnp.int32)
    hit = member[:, :, None] & (rank[:, :, None] == slot_range[None, None, :])
    source = jnp.sum(jnp.where(hit, token_range[:, None, None], 0), axis=0).reshape(-1)

    cot_send = pick_rows(cotangent, source)

    segment, offsets = segments_of(req_lengths[0], token_count)
    input32 = layer_input.astype(jnp.float32)
    input_scale = rms_scale(input32)
    normed = (input32 * input_scale * attn_gain[None, :]).astype(jnp.bfloat16)
    head_dim = key_proj.shape[1]
    cosine_table, sine_table = rope_tables(offsets, head_dim // 2)
    key_raw = jnp.dot(normed, key_proj, preferred_element_type=jnp.float32)
    key_normed = key_raw * rms_scale(key_raw) * key_gain
    key_rows = rotate(key_normed, cosine_table, sine_table).astype(jnp.bfloat16)
    value_rows = jnp.dot(normed, value_proj, preferred_element_type=jnp.float32)
    value_rows = value_rows.astype(jnp.bfloat16)
    places = jnp.arange(token_count, dtype=jnp.int32)
    allowed = (segment[:, None] == segment[None, :]) & (places[None, :] <= places[:, None])
    mask = allowed.astype(jnp.float32)
    cosines = jnp.concatenate([cosine_table, cosine_table], axis=1)
    sines = jnp.concatenate([-sine_table, sine_table], axis=1)
    query_gain2, key_gain2 = query_gain[None, :], key_gain[None, :]
    prep = (cot_send, query_w, normed, key_raw, key_rows, value_rows, cosines, sines, mask)
    prep = (*prep, flat_ids, flat_slots, router_row)
    prep = lax.optimization_barrier(prep)
    cot_send, query_w, normed, key_raw, key_rows, value_rows, cosines, sines, mask = prep[:9]
    flat_ids, flat_slots, router_row = prep[9:]
    cot_rows3 = exchange(cot_send, device_count)
    context, query_raw, attn_weights = attend(
        normed, query_w, key_rows, value_rows, cosines, sines, query_gain2, mask
    )
    other_rows = lax.dynamic_slice_in_dim(context, (1 - head_index) * moe_tokens, moe_tokens, 0)
    own_rows = lax.dynamic_slice_in_dim(context, head_index * moe_tokens, moe_tokens, 0)
    came = swap_heads(other_rows)
    context_tok = jnp.concatenate(
        [jnp.where(first_core, own_rows, came), jnp.where(first_core, came, own_rows)], axis=1
    )
    own_input = lax.dynamic_slice_in_dim(layer_input, head_index * moe_tokens, moe_tokens, 0)
    residual = own_input.astype(jnp.float32) + context_tok.astype(jnp.float32)
    moe_scale = rms_scale(residual)
    moe_in = (residual * moe_scale * moe_gain[None, :]).astype(jnp.bfloat16)
    moe_send = pick_rows(moe_in, source)
    rows3 = exchange(moe_send, device_count)

    logits = jnp.dot(moe_in, router, preferred_element_type=jnp.float32)
    chosen = jnp.sum(jnp.where(chosen_mask, logits[:, None, :], 0.0), axis=2)
    gates = jax.nn.softmax(chosen, axis=1)
    flat_gates = gates.reshape(-1)
    dense = jnp.sum(jnp.where(chosen_mask, gates[:, :, None], 0.0), axis=1)
    router_part = jnp.dot(
        dense, router.astype(jnp.float32).T, precision=lax.Precision.HIGHEST
    )
    router_part = lax.optimization_barrier(router_part)
    cot32 = cotangent.astype(jnp.float32)

    gate_w = w_gate[0]
    up_w = w_up[0]
    down_w = w_down[0]
    cot_rows = spread_rows(cot_rows3)
    cot_hidden = jnp.dot(cot_rows, down_w.T, preferred_element_type=jnp.float32)
    cot_hidden = lax.optimization_barrier(cot_hidden)
    grad_send, hidden = expert(rows3, gate_w, up_w, cot_hidden, router_row, device_count)
    grad_back = exchange(grad_send, device_count)
    outputs = jnp.dot(hidden, down_w, preferred_element_type=jnp.float32).astype(jnp.bfloat16)
    out_send = fold_rows(outputs, capacity)
    out_back = exchange(out_send, device_count)

    grad_sum, slot_sum = mix_rows(
        grad_back, flat_ids, flat_slots, flat_gates, None, router_part[:, :128], capacity
    )
    total_gate = slot_sum[:, :1] + slot_sum[:, 64:65]
    grad_in = grad_sum - total_gate * router_part
    grad_resid = cot32 + norm_backward(residual, moe_scale, moe_gain, grad_in)
    left, right = grad_resid[:, :half_width], grad_resid[:, half_width:]
    came_grad = swap_heads(jnp.where(first_core, right, left))
    own_grad = jnp.where(first_core, left, right)
    grad_heads = jnp.concatenate(
        [jnp.where(first_core, own_grad, came_grad), jnp.where(first_core, came_grad, own_grad)],
        axis=0,
    )
    query_grad, key_grad, value_grad = attend_back(
        grad_heads.astype(jnp.bfloat16),
        attn_weights,
        query_raw,
        key_rows,
        value_rows,
        key_raw,
        cosines,
        sines,
        query_gain2,
        key_gain2,
    )
    weights3 = (query_w, key_proj, value_proj)
    grads3 = (query_grad, key_grad, value_grad)
    other_half = project_back((1 - head_index)[None], *grads3, *weights3, jnp.bfloat16)
    came_half = swap_heads(other_half)
    own_half = project_back(head_index[None], *grads3, *weights3, jnp.float32)
    input_half = lax.dynamic_slice_in_dim(layer_input, head_index * half_width, half_width, 1)
    input_half = input_half.astype(jnp.float32)
    gain_half = lax.dynamic_slice_in_dim(attn_gain, head_index * half_width, half_width, 0)
    weighted = (own_half + came_half.astype(jnp.float32)) * gain_half[None, :]
    inner_part = jnp.sum(weighted * input_half, axis=1)
    direct_part = jnp.sum(grad_heads * input_half, axis=1)
    parts = jnp.stack([inner_part, direct_part], axis=0)
    inner_sum, direct_sum = parts + swap_heads(parts)
    inner = inner_sum[:, None] / width
    grad_attn = input_scale * weighted - input_half * input_scale**3 * inner
    attribution = (grad_heads + grad_attn) * input_half
    square_sum = jnp.sum(input32 * input32, axis=1)
    scale_row = input_scale[:, 0]
    token_score = direct_sum + (
        scale_row * inner_sum - scale_row**3 * (inner_sum / width) * square_sum
    )
    mixed = mix_rows(
        out_back, flat_ids, flat_slots, flat_gates, residual, own_half[:moe_tokens, :128], capacity
    )
    return (mixed, attribution, token_score)


def solution(mesh):
    return jax.shard_map(
        device_step,
        mesh=mesh,
        in_specs=(
            P("req", None),
            P("req", "head"),
            P(None, "head"),
            P(None, "head"),
            P(),
            P(),
            P(),
            P(),
            P(),
            P(("req", "head"), None),
            P("req", None),
            P(("req", "head"), None, None),
            P(("req", "head"), None, None),
            P(("req", "head"), None, None),
            P(("req", "head"), None),
        ),
        out_specs=(P(("req", "head"), None), P("req", "head"), P("req")),
        check_vma=False,
    )
```

```python
import functools
import math

import jax
import jax.numpy as jnp
from jax import lax
from jax.experimental import pallas as pl
from jax.experimental.pallas import tpu as pltpu
from jax.sharding import PartitionSpec as P


EPS = 1e-06
THETA = 1000000.0
NEG = -1e30


def segments_of(lengths_row, token_count):
    ends = jnp.cumsum(lengths_row)
    starts = ends - lengths_row
    places = jnp.arange(token_count, dtype=jnp.int32)
    segment = jnp.sum((places[:, None] >= ends[None, :]).astype(jnp.int32), axis=1)
    picked = (
        segment[:, None] == jnp.arange(lengths_row.shape[0], dtype=jnp.int32)[None, :]
    ).astype(jnp.int32)
    start_of = jnp.sum(picked * starts[None, :], axis=1)
    return (segment, places - start_of)


def rope_tables(offsets, half_dim):
    freq = THETA ** (-jnp.arange(half_dim, dtype=jnp.float32) / half_dim)
    angle = offsets.astype(jnp.float32)[:, None] * freq[None, :]
    return (jnp.cos(angle), jnp.sin(angle))


def rotate(rows, cosine_table, sine_table):
    half_dim = rows.shape[-1] // 2
    first = rows[..., :half_dim]
    second = rows[..., half_dim:]
    return jnp.concatenate(
        [first * cosine_table - second * sine_table, second * cosine_table + first * sine_table],
        axis=-1,
    )


def rms_scale(values):
    return lax.rsqrt(jnp.mean(values * values, axis=-1, keepdims=True) + EPS)


def norm_backward(values, scale, gain, grad_out):
    weighted = grad_out * gain
    inner = jnp.mean(weighted * values, axis=-1, keepdims=True)
    return scale * weighted - values * scale**3 * inner


SUB = 32
PART = 1024
VMEM_LIMIT = 56 * 1024 * 1024


def pick_kernel(index_ref, rows_ref, out_ref, folded):
    step_rows = out_ref.shape[0]
    base = pl.program_id(0) * step_rows

    @pl.when(pl.program_id(0) == 0)
    def _():
        folded[...] = rows_ref[...].reshape(folded.shape)

    def one(i, carry):
        out_ref[i] = folded[index_ref[base + i]]
        return carry

    lax.fori_loop(0, step_rows, one, 0, unroll=8)


def pick_rows(rows, index, step_rows=80):
    count = index.shape[0]
    tokens, width = rows.shape
    lanes = width // SUB
    return pl.pallas_call(
        pick_kernel,
        out_shape=jax.ShapeDtypeStruct((count, SUB, lanes), rows.dtype),
        grid_spec=pltpu.PrefetchScalarGridSpec(
            num_scalar_prefetch=1,
            grid=(count // step_rows,),
            in_specs=[pl.BlockSpec(rows.shape, lambda i, ids: (0, 0))],
            out_specs=pl.BlockSpec((step_rows, SUB, lanes), lambda i, ids: (i, 0, 0)),
            scratch_shapes=[pltpu.VMEM((tokens, SUB, lanes), rows.dtype)],
        ),
        cost_estimate=pl.CostEstimate(
            flops=0, transcendentals=0, bytes_accessed=count * width * 2
        ),
        name="pick_rows",
    )(index, rows)


def mix_block(id_ref, slot_ref, gate_ref, rows_ref, total):
    parts, tokens = total.shape[:2]
    top = id_ref.shape[0] // tokens
    per = rows_ref.shape[1] // parts

    def one(i, carry):
        sums = [None] * parts
        for k in range(top):
            at = i * top + k
            block, place, gate = id_ref[at], slot_ref[at], gate_ref[at]
            for p in range(parts):
                own = gate * rows_ref[block, place + p * per].astype(jnp.float32)
                sums[p] = own if k == 0 else sums[p] + own
        for p in range(parts):
            total[p, i] = sums[p]
        return carry

    lax.fori_loop(0, tokens, one, 0, unroll=2)


def mix_out_kernel(id_ref, slot_ref, gate_ref, rows_ref, base_ref, after_ref, out_ref, total):
    del after_ref
    mix_block(id_ref, slot_ref, gate_ref, rows_ref, total)
    parts, tokens, sub, lanes = total.shape
    for p in range(parts):
        at = slice(p * sub * lanes, (p + 1) * sub * lanes)
        mixed = base_ref[:, at] + total[p].reshape(tokens, sub * lanes)
        out_ref[:, at] = mixed.astype(out_ref.dtype)


def mix_grad_kernel(id_ref, slot_ref, gate_ref, rows_ref, extra_ref, after_ref, out_ref, sum_ref, total):
    del after_ref
    mix_block(id_ref, slot_ref, gate_ref, rows_ref, total)
    parts, tokens, sub, lanes = total.shape
    for p in range(parts):
        at = slice(p * sub * lanes, (p + 1) * sub * lanes)
        out_ref[:, at] = total[p].reshape(tokens, sub * lanes)
    top = id_ref.shape[0] // tokens

    @pl.when(pl.program_id(0) == 0)
    def _():
        line = lax.broadcasted_iota(jnp.int32, extra_ref.shape[2:], 0)

        def one(i, carry):
            tile = jnp.zeros(extra_ref.shape[2:], jnp.float32)
            for k in range(top):
                at = i * top + k
                own = gate_ref[at] * extra_ref[id_ref[at], 0].astype(jnp.float32)
                tile = tile + jnp.where(line == slot_ref[at], own, 0.0)
            sum_ref[pl.ds(i, 1), :] = jnp.sum(tile, axis=0, keepdims=True)
            return carry

        lax.fori_loop(0, tokens, one, 0, unroll=2)


def mix_rows(back4, ids, places, gates, base, after, capacity):
    blocks, _, sub, lanes = back4.shape
    top_tokens = ids.shape[0]
    tokens = after.shape[0]
    steps = 2
    parts = SUB // sub // steps
    part = parts * sub * lanes
    rows_spec = pl.BlockSpec((blocks, parts * capacity, sub, lanes), lambda k, *_: (0, k, 0, 0))
    wide = pl.BlockSpec((tokens, part), lambda k, *_: (0, k))
    flat = pl.BlockSpec((tokens, lanes), lambda k, *_: (0, 0))
    if base is None:
        extra = pl.BlockSpec((blocks, 1, sub, lanes), lambda k, *_: (0, steps * parts * capacity, 0, 0))
        kernel, specs, operands = mix_grad_kernel, [rows_spec, extra, flat], (back4, back4, after)
        out_shape = (
            jax.ShapeDtypeStruct((tokens, steps * part), jnp.float32),
            jax.ShapeDtypeStruct((tokens, lanes), jnp.float32),
        )
        out_specs = (wide, flat)
    else:
        kernel, specs, operands = mix_out_kernel, [rows_spec, wide, flat], (back4, base, after)
        out_shape = jax.ShapeDtypeStruct((tokens, steps * part), jnp.bfloat16)
        out_specs = wide
    return pl.pallas_call(
        kernel,
        out_shape=out_shape,
        grid_spec=pltpu.PrefetchScalarGridSpec(
            num_scalar_prefetch=3,
            grid=(steps,),
            in_specs=specs,
            out_specs=out_specs,
            scratch_shapes=[pltpu.VMEM((parts, tokens, sub, lanes), jnp.float32)],
        ),
        cost_estimate=pl.CostEstimate(
            flops=top_tokens * steps * part * 2,
            transcendentals=0,
            bytes_accessed=blocks * capacity * steps * part * 2,
        ),
        name="mix_rows",
    )(ids, places, gates, *operands)


def spread_kernel(rows_ref, out_ref):
    out_ref[...] = rows_ref[...].reshape(out_ref.shape)


def spread_rows(rows3, step_rows=128):
    count, sub, lanes = rows3.shape
    return pl.pallas_call(
        spread_kernel,
        out_shape=jax.ShapeDtypeStruct((count, sub * lanes), rows3.dtype),
        grid=(count // step_rows,),
        in_specs=[pl.BlockSpec((step_rows, sub, lanes), lambda i: (i, 0, 0))],
        out_specs=pl.BlockSpec((step_rows, sub * lanes), lambda i: (i, 0)),
        cost_estimate=pl.CostEstimate(
            flops=0, transcendentals=0, bytes_accessed=4 * count * sub * lanes
        ),
        name="spread_rows",
    )(rows3)


def fold_kernel(rows_ref, out_ref):
    blocks, places, sub, lanes = out_ref.shape
    part = sub * lanes
    parts = rows_ref.shape[1] // part
    per = places // parts
    for k in range(parts):
        rows = rows_ref[:, k * part : (k + 1) * part]
        out_ref[:, k * per : (k + 1) * per] = rows.reshape(blocks, per, sub, lanes)


def fold_rows(rows, capacity, step_blocks=32):
    count, width = rows.shape
    blocks = count // capacity
    places = capacity * width // PART
    return pl.pallas_call(
        fold_kernel,
        out_shape=jax.ShapeDtypeStruct((blocks, places, 8, PART // 8), jnp.bfloat16),
        grid=(blocks // step_blocks,),
        in_specs=[pl.BlockSpec((step_blocks * capacity, width), lambda i: (i, 0))],
        out_specs=pl.BlockSpec((step_blocks, places, 8, PART // 8), lambda i: (i, 0, 0, 0)),
        cost_estimate=pl.CostEstimate(
            flops=0, transcendentals=0, bytes_accessed=4 * count * width
        ),
        name="fold_rows",
    )(rows)


VM = pl.BlockSpec(memory_space=pltpu.VMEM)
NT = (((1,), (1,)), ((), ()))
TN = (((0,), (0,)), ((), ()))


def turn(rows, cosines, sines):
    return rows * cosines + pltpu.roll(rows, rows.shape[1] // 2, 1) * sines


def unturn(rows, cosines, sines):
    return rows * cosines - pltpu.roll(rows, rows.shape[1] // 2, 1) * sines


def attend_kernel(
    normed_ref,
    query_w_ref,
    key_ref,
    value_ref,
    cos_ref,
    sin_ref,
    gain_ref,
    mask_ref,
    context_ref,
    raw_ref,
    weight_ref,
    held,
):
    step = pl.program_id(0)
    head_dim = key_ref.shape[1]
    heads = query_w_ref.shape[1] // head_dim

    @pl.when(step == 0)
    def _():
        held[...] = jnp.zeros_like(held)

    ready = held.at[lax.rem(step + 1, 2)]
    raw = ready[...]
    raw_ref[...] = raw
    held[lax.rem(step, 2)] = jnp.dot(
        normed_ref[...], query_w_ref[...], preferred_element_type=jnp.float32
    )
    factor = 1.0 / math.sqrt(head_dim)
    for g in range(heads):
        cols = slice(g * head_dim, (g + 1) * head_dim)
        own = raw[:, cols]
        scale = lax.rsqrt(jnp.sum(own * own, axis=1, keepdims=True) / head_dim + EPS)
        rows = turn(own * scale * gain_ref[...], cos_ref[...], sin_ref[...]).astype(jnp.bfloat16)
        scores = lax.dot_general(rows, key_ref[...], NT, preferred_element_type=jnp.float32)
        terms = jnp.exp(jnp.where(mask_ref[...] > 0.0, scores * factor, NEG))
        weights = terms / jnp.sum(terms, axis=1, keepdims=True)
        weight_ref[:, cols] = weights
        context = jnp.dot(
            weights.astype(jnp.bfloat16), value_ref[...], preferred_element_type=jnp.float32
        )
        context_ref[:, cols] = context.astype(jnp.bfloat16)


def attend(normed, query_w, key_rows, value_rows, cosines, sines, gain, mask, block=256):
    tokens, width = normed.shape
    columns = query_w.shape[1]
    steps = columns // block
    late = pl.BlockSpec((tokens, block), lambda i: (0, jnp.maximum(i - 1, 0)))
    whole = lambda a: pl.BlockSpec(a.shape, lambda i: (0, 0))
    return pl.pallas_call(
        attend_kernel,
        out_shape=(
            jax.ShapeDtypeStruct((tokens, columns), jnp.bfloat16),
            jax.ShapeDtypeStruct((tokens, columns), jnp.float32),
            jax.ShapeDtypeStruct((tokens, columns), jnp.float32),
        ),
        grid=(steps + 1,),
        in_specs=[
            whole(normed),
            pl.BlockSpec((width, block), lambda i: (0, jnp.minimum(i, steps - 1))),
            whole(key_rows),
            whole(value_rows),
            whole(cosines),
            whole(sines),
            whole(gain),
            whole(mask),
        ],
        out_specs=(late, late, late),
        scratch_shapes=[pltpu.VMEM((2, tokens, block), jnp.float32)],
        cost_estimate=pl.CostEstimate(
            flops=2 * tokens * width * columns,
            transcendentals=0,
            bytes_accessed=2 * width * columns,
        ),
        name="attend",
    )(normed, query_w, key_rows, value_rows, cosines, sines, gain, mask)


def attend_back_kernel(
    grad_ref,
    weight_ref,
    raw_ref,
    key_ref,
    value_ref,
    key_raw_ref,
    cos_ref,
    sin_ref,
    gain_ref,
    key_gain_ref,
    query_out,
    key_out,
    value_out,
    key_sum,
    value_sum,
):
    step = pl.program_id(0)
    head_dim = key_ref.shape[1]
    heads = grad_ref.shape[1] // head_dim
    factor = 1.0 / math.sqrt(head_dim)
    cosines, sines, gain = cos_ref[...], sin_ref[...], gain_ref[...]

    @pl.when(step == 0)
    def _():
        key_sum[...] = jnp.zeros_like(key_sum)
        value_sum[...] = jnp.zeros_like(value_sum)

    key_total, value_total = key_sum[...], value_sum[...]
    for g in range(heads):
        cols = slice(g * head_dim, (g + 1) * head_dim)
        grad = grad_ref[:, cols]
        weights = weight_ref[:, cols]
        own = raw_ref[:, cols]
        scale = lax.rsqrt(jnp.sum(own * own, axis=1, keepdims=True) / head_dim + EPS)
        rows = turn(own * scale * gain, cosines, sines).astype(jnp.bfloat16)
        grad_weights = lax.dot_general(grad, value_ref[...], NT, preferred_element_type=jnp.float32)
        value_total += lax.dot_general(
            weights.astype(jnp.bfloat16), grad, TN, preferred_element_type=jnp.float32
        )
        centered = grad_weights - jnp.sum(grad_weights * weights, axis=1, keepdims=True)
        grad_scores = (weights * centered * factor).astype(jnp.bfloat16)
        key_total += lax.dot_general(grad_scores, rows, TN, preferred_element_type=jnp.float32)
        grad_rows = jnp.dot(grad_scores, key_ref[...], preferred_element_type=jnp.float32)
        weighted = unturn(grad_rows, cosines, sines) * gain
        inner = jnp.sum(weighted * own, axis=1, keepdims=True) / head_dim
        query_out[:, cols] = (scale * weighted - own * (scale * scale * scale) * inner).astype(
            jnp.bfloat16
        )
    key_sum[...] = key_total
    value_sum[...] = value_total

    @pl.when(step == pl.num_programs(0) - 1)
    def _():
        own = key_raw_ref[...]
        scale = lax.rsqrt(jnp.sum(own * own, axis=1, keepdims=True) / head_dim + EPS)
        weighted = unturn(key_sum[...], cosines, sines) * key_gain_ref[...]
        inner = jnp.sum(weighted * own, axis=1, keepdims=True) / head_dim
        key_out[...] = (scale * weighted - own * (scale * scale * scale) * inner).astype(
            jnp.bfloat16
        )
        value_out[...] = value_sum[...].astype(jnp.bfloat16)


def attend_back(
    grad, weights, raw, key_rows, value_rows, key_raw, cosines, sines, gain, key_gain, block=512
):
    tokens, columns = grad.shape
    head_dim = key_rows.shape[1]
    piece = pl.BlockSpec((tokens, block), lambda i: (0, i))
    whole = lambda a: pl.BlockSpec(a.shape, lambda i: (0, 0))
    small = pl.BlockSpec((tokens, head_dim), lambda i: (0, 0))
    rest = (key_rows, value_rows, key_raw, cosines, sines, gain, key_gain)
    return pl.pallas_call(
        attend_back_kernel,
        out_shape=(
            jax.ShapeDtypeStruct((tokens, columns), jnp.bfloat16),
            jax.ShapeDtypeStruct((tokens, head_dim), jnp.bfloat16),
            jax.ShapeDtypeStruct((tokens, head_dim), jnp.bfloat16),
        ),
        grid=(columns // block,),
        in_specs=[piece, piece, piece, *map(whole, rest)],
        out_specs=(piece, small, small),
        scratch_shapes=[pltpu.VMEM((tokens, head_dim), jnp.float32)] * 2,
        cost_estimate=pl.CostEstimate(
            flops=12 * tokens * tokens * columns,
            transcendentals=0,
            bytes_accessed=12 * tokens * columns,
        ),
        name="attend_back",
    )(grad, weights, raw, *rest)


def project_kernel(at_ref, query_ref, key_ref, value_ref, query_w, key_w, value_w, out_ref):
    del at_ref
    total = lax.dot_general(query_ref[...], query_w[...], NT, preferred_element_type=jnp.float32)
    total += lax.dot_general(key_ref[...], key_w[...], NT, preferred_element_type=jnp.float32)
    total += lax.dot_general(value_ref[...], value_w[...], NT, preferred_element_type=jnp.float32)
    out_ref[...] = total.astype(out_ref.dtype)


def project_back(part, query_grad, key_grad, value_grad, query_w, key_w, value_w, dtype, block=512):
    tokens, columns = query_grad.shape
    width, _ = key_w.shape
    steps = width // 2 // block
    whole = lambda a: pl.BlockSpec(a.shape, lambda i, at: (0, 0))
    rows = lambda a: pl.BlockSpec((block, a.shape[1]), lambda i, at: (at[0] * steps + i, 0))
    return pl.pallas_call(
        project_kernel,
        out_shape=jax.ShapeDtypeStruct((tokens, width // 2), dtype),
        grid_spec=pltpu.PrefetchScalarGridSpec(
            num_scalar_prefetch=1,
            grid=(steps,),
            in_specs=[
                whole(query_grad),
                whole(key_grad),
                whole(value_grad),
                rows(query_w),
                rows(key_w),
                rows(value_w),
            ],
            out_specs=pl.BlockSpec((tokens, block), lambda i, at: (0, i)),
        ),
        cost_estimate=pl.CostEstimate(
            flops=tokens * columns * width,
            transcendentals=0,
            bytes_accessed=columns * width,
        ),
        name="project_back",
    )(part, query_grad, key_grad, value_grad, query_w, key_w, value_w)


def expert_kernel(
    rows_hbm,
    gate_hbm,
    up_hbm,
    cot_hbm,
    router_ref,
    grad_hbm,
    hidden_ref,
    rows_v,
    made_v,
    extra_v,
    slot_v,
    gate_w,
    up_w,
    cot_ref,
    pre_gate,
    pre_up,
    grad_gate,
    grad_up,
    sem_in,
    sem_gate,
    sem_up,
    sem_cot,
    sem_out,
    sem_extra,
    *,
    chunks,
    row_block,
):
    count, piece, lanes = rows_v.shape[1:]
    part = piece * lanes

    def arrive(k, place):
        at = pl.ds(place * piece, piece)
        return pltpu.make_async_copy(rows_hbm.at[:, at, :], rows_v.at[k], sem_in.at[k])

    blocks, per = made_v.shape[1:3]

    def leave(k):
        at = pl.ds(k * per, per)
        return pltpu.make_async_copy(made_v.at[k], grad_hbm.at[:, at], sem_out.at[k])

    leave_extra = pltpu.make_async_copy(extra_v, grad_hbm.at[:, chunks * per], sem_extra)

    def gate_in(k):
        at = pl.ds(pl.multiple_of(k * part, part), part)
        return pltpu.make_async_copy(gate_hbm.at[at, :], gate_w.at[at, :], sem_gate.at[k])

    def up_in(k):
        at = pl.ds(pl.multiple_of(k * part, part), part)
        return pltpu.make_async_copy(up_hbm.at[at, :], up_w.at[at, :], sem_up.at[k])

    cot_in = pltpu.make_async_copy(cot_hbm, cot_ref, sem_cot)
    for k in range(chunks):
        arrive(k, k).start()
        gate_in(k).start()
        up_in(k).start()
    cot_in.start()
    pre_gate[...] = jnp.zeros_like(pre_gate)
    pre_up[...] = jnp.zeros_like(pre_up)

    def ahead(k, carry):
        arrive(k, 0).wait()
        gate_in(k).wait()
        up_in(k).wait()
        rows = rows_v[k].reshape(count, part)
        at = pl.ds(pl.multiple_of(k * part, part), part)
        pre_gate[...] += jnp.dot(rows, gate_w[at, :], preferred_element_type=jnp.float32)
        pre_up[...] += jnp.dot(rows, up_w[at, :], preferred_element_type=jnp.float32)
        return carry

    lax.fori_loop(0, chunks, ahead, 0)
    cot_in.wait()

    def between(r, carry):
        at = pl.ds(pl.multiple_of(r * row_block, 16), row_block)
        gate, up, cot = pre_gate[at, :], pre_up[at, :], cot_ref[at, :]
        sigmoid = 1.0 / (1.0 + jnp.exp(-gate))
        silu = gate * sigmoid
        hidden = (silu * up).astype(jnp.bfloat16)
        hidden_ref[at, :] = hidden
        grad_up[at, :] = (cot * silu).astype(jnp.bfloat16)
        grad_gate[at, :] = (cot * up * sigmoid * (1.0 + gate * (1.0 - sigmoid))).astype(
            jnp.bfloat16
        )
        slot = jnp.sum(hidden.astype(jnp.float32) * cot, axis=1, keepdims=True)
        slot_v[at, :] = jnp.broadcast_to(slot, (row_block, slot_v.shape[1]))
        return carry

    lax.fori_loop(0, count // row_block, between, 0)

    def behind(k, carry):
        at = pl.ds(pl.multiple_of(k * part, part), part)
        grad = lax.dot_general(grad_gate[...], gate_w[at, :], NT, preferred_element_type=jnp.float32)
        grad += lax.dot_general(grad_up[...], up_w[at, :], NT, preferred_element_type=jnp.float32)
        grad += slot_v[:, :1] * router_ref[:, at]
        made_v[k] = grad.astype(jnp.bfloat16).reshape(
            blocks, per, piece, lanes
        )
        leave(k).start()
        return carry

    lax.fori_loop(0, chunks, behind, 0)
    slot = slot_v[...]
    upper = slot.astype(jnp.bfloat16)
    lower = (slot - upper.astype(jnp.float32)).astype(jnp.bfloat16)
    lane = lax.broadcasted_iota(jnp.int32, slot.shape, 1)
    value = jnp.where(lane < lanes // 2, upper.astype(jnp.float32), lower.astype(jnp.float32))
    value = value.astype(jnp.bfloat16)
    group = 16
    column = lax.broadcasted_iota(jnp.int32, (group * 8, count), 1)
    line = lax.broadcasted_iota(jnp.int32, (group * 8, count), 0)
    for b in range(0, blocks, group):
        block, place = lax.shift_right_logical(line, 3) + b, line & 7
        select = jnp.where((block * per + place == column) & (place < per), 1.0, 0.0)
        extra = jnp.dot(select.astype(jnp.bfloat16), value, preferred_element_type=jnp.float32)
        extra_v[b : b + group] = extra.astype(jnp.bfloat16).reshape(group, 8, lanes)
    leave_extra.start()
    for k in range(chunks):
        leave(k).wait()
    leave_extra.wait()


def expert(rows3, gate_w, up_w, cot_hidden, router_row, blocks, chunks=4, row_block=80):
    count, sub, lanes = rows3.shape
    made = (blocks, chunks * count // blocks + 1, sub // chunks, lanes)
    inner = gate_w.shape[1]
    hbm = pl.BlockSpec(memory_space=pltpu.HBM)
    return pl.pallas_call(
        functools.partial(expert_kernel, chunks=chunks, row_block=row_block),
        out_shape=(
            jax.ShapeDtypeStruct(made, jnp.bfloat16),
            jax.ShapeDtypeStruct((count, inner), jnp.bfloat16),
        ),
        in_specs=[hbm, hbm, hbm, hbm, VM],
        out_specs=(hbm, VM),
        scratch_shapes=[
            pltpu.VMEM((chunks, count, sub // chunks, lanes), jnp.bfloat16),
            pltpu.VMEM((chunks, blocks, count // blocks, *made[2:]), jnp.bfloat16),
            pltpu.VMEM((blocks, *made[2:]), jnp.bfloat16),
            pltpu.VMEM((count, lanes), jnp.float32),
            pltpu.VMEM(gate_w.shape, jnp.bfloat16),
            pltpu.VMEM(up_w.shape, jnp.bfloat16),
            pltpu.VMEM((count, inner), jnp.float32),
            pltpu.VMEM((count, inner), jnp.float32),
            pltpu.VMEM((count, inner), jnp.float32),
            pltpu.VMEM((count, inner), jnp.bfloat16),
            pltpu.VMEM((count, inner), jnp.bfloat16),
            pltpu.SemaphoreType.DMA((chunks,)),
            pltpu.SemaphoreType.DMA((chunks,)),
            pltpu.SemaphoreType.DMA((chunks,)),
            pltpu.SemaphoreType.DMA,
            pltpu.SemaphoreType.DMA((chunks,)),
            pltpu.SemaphoreType.DMA,
        ],
        compiler_params=pltpu.CompilerParams(vmem_limit_bytes=VMEM_LIMIT),
        cost_estimate=pl.CostEstimate(
            flops=8 * count * inner * gate_w.shape[0],
            transcendentals=0,
            bytes_accessed=4 * rows3.shape[0] * gate_w.shape[0],
        ),
        name="expert",
    )(rows3, gate_w, up_w, cot_hidden, router_row)


def swap_heads(values):
    return lax.ppermute(values, "head", [(0, 1), (1, 0)])


def exchange(rows, device_count):
    packed = rows.reshape(device_count, -1, 128)
    moved = lax.all_to_all(packed, ("req", "head"), split_axis=0, concat_axis=0, tiled=True)
    return moved.reshape(rows.shape)


def device_step(
    layer_input,
    q_proj,
    key_proj,
    value_proj,
    query_gain,
    key_gain,
    attn_gain,
    moe_gain,
    router,
    expert_ids,
    req_lengths,
    w_gate,
    w_up,
    w_down,
    cotangent,
):
    head_count = lax.axis_size("head")
    head_index = lax.axis_index("head")
    device_count = lax.axis_size("req") * head_count
    token_count, width = layer_input.shape
    moe_tokens = token_count // head_count
    half_width = width // head_count
    capacity = 5
    first_core = head_index == 0

    query_w = lax.all_gather(q_proj, "req", axis=0, tiled=True)

    expert_range = jnp.arange(device_count, dtype=jnp.int32)
    chosen_mask = expert_ids[:, :, None] == expert_range[None, None, :]
    member = jnp.any(chosen_mask, axis=1)
    token_range = jnp.arange(moe_tokens, dtype=jnp.int32)
    before = (token_range[:, None] > token_range[None, :]).astype(jnp.bfloat16)
    rank = jnp.dot(before, member.astype(jnp.bfloat16), preferred_element_type=jnp.float32)
    rank = rank.astype(jnp.int32)
    slot_of = jnp.sum(jnp.where(chosen_mask, rank[:, None, :], 0), axis=2)
    flat_ids, flat_slots = expert_ids.reshape(-1), slot_of.reshape(-1)
    device_index = lax.axis_index("req") * head_count + head_index
    router_row = lax.dynamic_slice_in_dim(router, device_index, 1, 1).astype(jnp.float32).T
    slot_range = jnp.arange(capacity, dtype=jnp.int32)
    hit = member[:, :, None] & (rank[:, :, None] == slot_range[None, None, :])
    source = jnp.sum(jnp.where(hit, token_range[:, None, None], 0), axis=0).reshape(-1)

    cot_send = pick_rows(cotangent, source)

    segment, offsets = segments_of(req_lengths[0], token_count)
    input32 = layer_input.astype(jnp.float32)
    input_scale = rms_scale(input32)
    normed = (input32 * input_scale * attn_gain[None, :]).astype(jnp.bfloat16)
    head_dim = key_proj.shape[1]
    cosine_table, sine_table = rope_tables(offsets, head_dim // 2)
    key_raw = jnp.dot(normed, key_proj, preferred_element_type=jnp.float32)
    key_normed = key_raw * rms_scale(key_raw) * key_gain
    key_rows = rotate(key_normed, cosine_table, sine_table).astype(jnp.bfloat16)
    value_rows = jnp.dot(normed, value_proj, preferred_element_type=jnp.float32)
    value_rows = value_rows.astype(jnp.bfloat16)
    places = jnp.arange(token_count, dtype=jnp.int32)
    allowed = (segment[:, None] == segment[None, :]) & (places[None, :] <= places[:, None])
    mask = allowed.astype(jnp.float32)
    cosines = jnp.concatenate([cosine_table, cosine_table], axis=1)
    sines = jnp.concatenate([-sine_table, sine_table], axis=1)
    query_gain2, key_gain2 = query_gain[None, :], key_gain[None, :]
    prep = (cot_send, query_w, normed, key_raw, key_rows, value_rows, cosines, sines, mask)
    prep = (*prep, flat_ids, flat_slots, router_row)
    prep = lax.optimization_barrier(prep)
    cot_send, query_w, normed, key_raw, key_rows, value_rows, cosines, sines, mask = prep[:9]
    flat_ids, flat_slots, router_row = prep[9:]
    cot_rows3 = exchange(cot_send, device_count)
    context, query_raw, attn_weights = attend(
        normed, query_w, key_rows, value_rows, cosines, sines, query_gain2, mask
    )
    other_rows = lax.dynamic_slice_in_dim(context, (1 - head_index) * moe_tokens, moe_tokens, 0)
    own_rows = lax.dynamic_slice_in_dim(context, head_index * moe_tokens, moe_tokens, 0)
    came = swap_heads(other_rows)
    context_tok = jnp.concatenate(
        [jnp.where(first_core, own_rows, came), jnp.where(first_core, came, own_rows)], axis=1
    )
    own_input = lax.dynamic_slice_in_dim(layer_input, head_index * moe_tokens, moe_tokens, 0)
    residual = own_input.astype(jnp.float32) + context_tok.astype(jnp.float32)
    moe_scale = rms_scale(residual)
    moe_in = (residual * moe_scale * moe_gain[None, :]).astype(jnp.bfloat16)
    moe_send = pick_rows(moe_in, source)
    rows3 = exchange(moe_send, device_count)

    logits = jnp.dot(moe_in, router, preferred_element_type=jnp.float32)
    chosen = jnp.sum(jnp.where(chosen_mask, logits[:, None, :], 0.0), axis=2)
    gates = jax.nn.softmax(chosen, axis=1)
    flat_gates = gates.reshape(-1)
    dense = jnp.sum(jnp.where(chosen_mask, gates[:, :, None], 0.0), axis=1)
    router_part = jnp.dot(
        dense, router.astype(jnp.float32).T, precision=lax.Precision.HIGHEST
    )
    router_part = lax.optimization_barrier(router_part)
    cot32 = cotangent.astype(jnp.float32)

    gate_w = w_gate[0]
    up_w = w_up[0]
    down_w = w_down[0]
    cot_rows = spread_rows(cot_rows3)
    cot_hidden = jnp.dot(cot_rows, down_w.T, preferred_element_type=jnp.float32)
    cot_hidden = lax.optimization_barrier(cot_hidden)
    grad_send, hidden = expert(rows3, gate_w, up_w, cot_hidden, router_row, device_count)
    grad_back = exchange(grad_send, device_count)
    outputs = jnp.dot(hidden, down_w, preferred_element_type=jnp.float32).astype(jnp.bfloat16)
    out_send = fold_rows(outputs, capacity)
    out_back = exchange(out_send, device_count)

    grad_sum, slot_sum = mix_rows(
        grad_back, flat_ids, flat_slots, flat_gates, None, router_part[:, :128], capacity
    )
    total_gate = slot_sum[:, :1] + slot_sum[:, 64:65]
    grad_in = grad_sum - total_gate * router_part
    grad_resid = cot32 + norm_backward(residual, moe_scale, moe_gain, grad_in)
    left, right = grad_resid[:, :half_width], grad_resid[:, half_width:]
    came_grad = swap_heads(jnp.where(first_core, right, left))
    own_grad = jnp.where(first_core, left, right)
    grad_heads = jnp.concatenate(
        [jnp.where(first_core, own_grad, came_grad), jnp.where(first_core, came_grad, own_grad)],
        axis=0,
    )
    query_grad, key_grad, value_grad = attend_back(
        grad_heads.astype(jnp.bfloat16),
        attn_weights,
        query_raw,
        key_rows,
        value_rows,
        key_raw,
        cosines,
        sines,
        query_gain2,
        key_gain2,
    )
    weights3 = (query_w, key_proj, value_proj)
    grads3 = (query_grad, key_grad, value_grad)
    other_half = project_back((1 - head_index)[None], *grads3, *weights3, jnp.bfloat16)
    came_half = swap_heads(other_half)
    own_half = project_back(head_index[None], *grads3, *weights3, jnp.float32)
    input_half = lax.dynamic_slice_in_dim(layer_input, head_index * half_width, half_width, 1)
    input_half = input_half.astype(jnp.float32)
    gain_half = lax.dynamic_slice_in_dim(attn_gain, head_index * half_width, half_width, 0)
    weighted = (own_half + came_half.astype(jnp.float32)) * gain_half[None, :]
    inner_part = jnp.sum(weighted * input_half, axis=1)
    direct_part = jnp.sum(grad_heads * input_half, axis=1)
    parts = jnp.stack([inner_part, direct_part], axis=0)
    inner_sum, direct_sum = parts + swap_heads(parts)
    inner = inner_sum[:, None] / width
    grad_attn = input_scale * weighted - input_half * input_scale**3 * inner
    attribution = (grad_heads + grad_attn) * input_half
    square_sum = jnp.sum(input32 * input32, axis=1)
    scale_row = input_scale[:, 0]
    token_score = direct_sum + (
        scale_row * inner_sum - scale_row**3 * (inner_sum / width) * square_sum
    )
    mixed = mix_rows(
        out_back, flat_ids, flat_slots, flat_gates, residual, own_half[:moe_tokens, :128], capacity
    )
    return (mixed, attribution, token_score)


def solution(mesh):
    return jax.shard_map(
        device_step,
        mesh=mesh,
        in_specs=(
            P("req", None),
            P("req", "head"),
            P(None, "head"),
            P(None, "head"),
            P(),
            P(),
            P(),
            P(),
            P(),
            P(("req", "head"), None),
            P("req", None),
            P(("req", "head"), None, None),
            P(("req", "head"), None, None),
            P(("req", "head"), None, None),
            P(("req", "head"), None),
        ),
        out_specs=(P(("req", "head"), None), P("req", "head"), P("req")),
        check_vma=False,
    )
```
